32 devices in a mesh: dp: 4 (over z), seq: 8 (over y, x, core).
Axes of the slice: x: 2, y: 2, z: 4, core: 2. Of those that a mesh axis runs over, the one named last changes fastest.
Arguments:
- tokens: bfloat16 [8, 1024, 2048], P('dp', 'seq'), may hold values from -6 to 6
- cotangent: bfloat16 [8, 1024, 2048], P('dp', 'seq'), may hold values from -6 to 6
- lengths: int32 [8], replicated, may hold values from 1 to 1024, 6656 in all
- owner_order: int32 [8], replicated, may hold values from 0 to 7, each once
- first_gain: bfloat16 [2048], P(('dp', 'seq')), may hold values from 0.5 to 1.5
- first_bias: bfloat16 [2048], P(('dp', 'seq')), may hold values from -3 to 3
- w_query: bfloat16 [2048, 2048], P(('dp', 'seq')), may hold values from -0.125 to 0.125
- b_query: bfloat16 [2048], P(('dp', 'seq')), may hold values from -3 to 3
- w_keyval: bfloat16 [2048, 256], P(('dp', 'seq')), may hold values from -0.25 to 0.25
- b_value: bfloat16 [128], P(('dp', 'seq')), may hold values from -3 to 3
- w_out: bfloat16 [2048, 2048], P(('dp', 'seq')), may hold values from -1 to 1
- b_out: bfloat16 [2048], P(('dp', 'seq')), may hold values from -3 to 3
- second_gain: bfloat16 [2048], P(('dp', 'seq')), may hold values from 0.5 to 1.5
- second_bias: bfloat16 [2048], P(('dp', 'seq')), may hold values from -3 to 3
- w_expand: bfloat16 [2048, 8192], P(('dp', 'seq')), may hold values from -0.125 to 0.125
- b_expand: bfloat16 [8192], P(('dp', 'seq')), may hold values from -3 to 3
- w_contract: bfloat16 [8192, 2048], P(('dp', 'seq')), may hold values from -0.0625 to 0.0625
- b_contract: bfloat16 [2048], P(('dp', 'seq')), may hold values from -3 to 3
Outputs:
- result: bfloat16 [8, 1024, 2048], P('dp', 'seq')
- grad_tokens: float32 [8, 1024, 2048], P('dp', 'seq')
- grad_first_gain: float32 [2048], P(('dp', 'seq'))
- grad_first_bias: float32 [2048], P(('dp', 'seq'))
- grad_w_query: float32 [2048, 2048], P(('dp', 'seq'))
- grad_b_query: float32 [2048], P(('dp', 'seq'))
- grad_w_keyval: float32 [2048, 256], P(('dp', 'seq'))
- grad_b_value: float32 [128], P(('dp', 'seq'))
- grad_w_out: float32 [2048, 2048], P(('dp', 'seq'))
- grad_b_out: float32 [2048], P(('dp', 'seq'))
- grad_second_gain: float32 [2048], P(('dp', 'seq'))
- grad_second_bias: float32 [2048], P(('dp', 'seq'))
- grad_w_expand: float32 [2048, 8192], P(('dp', 'seq'))
- grad_b_expand: float32 [8192], P(('dp', 'seq'))
- grad_w_contract: float32 [8192, 2048], P(('dp', 'seq'))
- grad_b_contract: float32 [2048], P(('dp', 'seq'))
The draws below stay inside these ranges and needn't reach their ends.
Inputs may be any that keep to these rules, and one draw needn't show every extreme that they name: `lengths`: each sequence has 1 to 1024 valid tokens, 6656 in all; at least one has 1024. `owner_order`: each sequence number appears exactly once.
All inputs are finite; a program needn't handle non-finite values.
Results may differ from the reference program's by a relative error of at most 0.011.
The reference program's roundings to bfloat16 on the way count: a program that leaves them out, or rounds other values in their place, can miss the bound.
Values may be sent and summed in bfloat16 or wider, within the bound.
No kernel may reach another device: no remote copies, remote signals or barrier semaphores. Data moves between devices by JAX's collectives and lax.ppermute only.
A program may use at most 384 MiB of HBM per device.

```python
import math
import jax
import jax.numpy as jnp
import numpy as np
from jax import lax

D = 2048
HEADS = 16
HD = 128
FF = 8192
NSEQ = 8
SLOT = 1024
VALID = 6656


def levels(key, extent, split, low, top_value):
    level = 1.0
    for axis_at, blocks in split:
        heights = jax.random.uniform(jax.random.fold_in(jax.random.fold_in(key, 6), axis_at), (blocks,), jnp.float32, low / len(split), top_value / len(split))
        level = level * jnp.repeat(jnp.exp(heights), extent[axis_at] // blocks).reshape((-1,) + (1,) * (len(extent) - 1 - axis_at))
    return level


def profile(amount, total, bound, skew):
    portions = [(1 << 20) // math.isqrt(standing ** skew) + 1 for standing in range(2, amount + 1)]
    surplus, counts = total - bound - (amount - 1), [1] * (amount - 1)
    while surplus > 0:
        candidates = [i for i in range(amount - 1) if counts[i] < bound]
        pool, left = sum([portions[i] for i in candidates]), surplus
        for i in candidates:
            extra = min(bound - counts[i], max(1, left * portions[i] // pool), surplus)
            counts[i] = counts[i] + extra
            surplus = surplus - extra
    return np.array([bound] + counts)


def ragged_sizes(key, number_of, total, bound, skew):
    if number_of == 2:
        one = jax.random.randint(key, (), max(1, total - bound), min(bound, total - 1) + 1)
        return jnp.stack([one, total - one])
    sizes = jnp.asarray(profile(number_of, total, bound, skew), jnp.int32)
    twos = (number_of - 1) // 2
    source_of, receiver = sizes[1:1 + 2 * twos:2], sizes[2:2 + 2 * twos:2]
    margin = jnp.minimum(source_of - 1, bound - receiver)
    passed = jax.random.randint(jax.random.fold_in(key, 1), (twos,), 0, 1 << 20) % (margin + 1)
    sizes = sizes.at[1:1 + 2 * twos:2].set(source_of - passed).at[2:2 + 2 * twos:2].set(receiver + passed)
    return sizes[jax.random.permutation(jax.random.fold_in(key, 2), number_of)]


def noise(stream_key, dims, width, most, pieces=(), kind=jnp.bfloat16):
    values = width * jax.random.normal(stream_key, dims, jnp.float32)
    if pieces:
        values = values * levels(stream_key, dims, pieces, -0.22, 0.18)
    return jnp.clip(values, -most, most).astype(kind)


def setup_inputs(seed: int = 0) -> dict:
    splits = jax.random.split(jax.random.key(seed), 19)
    return {
        "tokens": noise(splits[0], (NSEQ, SLOT, D), 1.0, 6.0, ((0, 4), (1, 8))),
        "cotangent": noise(splits[1], (NSEQ, SLOT, D), 1.0, 6.0, ((0, 4), (1, 8))),
        "lengths": ragged_sizes(splits[2], NSEQ, VALID, SLOT, 2).astype(jnp.int32),
        "owner_order": jax.random.permutation(splits[3], NSEQ).astype(jnp.int32),
        "first_gain": jnp.clip(1.0 + 0.1 * jax.random.normal(splits[4], (D,), jnp.float32), 0.5, 1.5).astype(jnp.bfloat16),
        "first_bias": noise(splits[5], (D,), 0.3, 3.0, ((0, 32),)),
        "w_query": noise(splits[6], (D, D), D ** -0.5, 0.125, ((0, 32),)),
        "b_query": noise(splits[7], (D,), 0.3, 3.0, ((0, 32),)),
        "w_keyval": noise(splits[8], (D, 2 * HD), (D // 4) ** -0.5, 0.25, ((0, 32),)),
        "b_value": noise(splits[9], (HD,), 0.3, 3.0, ((0, 32),)),
        "w_out": noise(splits[10], (D, D), (D // 64) ** -0.5, 1.0, ((0, 32),)),
        "b_out": noise(splits[11], (D,), 0.3, 3.0, ((0, 32),)),
        "second_gain": jnp.clip(1.0 + 0.1 * jax.random.normal(splits[12], (D,), jnp.float32), 0.5, 1.5).astype(jnp.bfloat16),
        "second_bias": noise(splits[13], (D,), 0.3, 3.0, ((0, 32),)),
        "w_expand": noise(splits[14], (D, FF), D ** -0.5, 0.125, ((0, 32),)),
        "b_expand": noise(splits[15], (FF,), 0.3, 3.0, ((0, 32),)),
        "w_contract": noise(splits[16], (FF, D), FF ** -0.5, 0.0625, ((0, 32),)),
        "b_contract": noise(splits[17], (D,), 0.3, 3.0, ((0, 32),)),
    }


@jax.custom_vjp
def low(v):
    return lax.optimization_barrier(v.astype(jnp.bfloat16)).astype(jnp.float32)

@jax.custom_vjp
def low_back(v):
    return v

def low_keep(v):
    return (low(v), None)

def low_pass(kept, grad):
    return (grad,)

def back_keep(v):
    return (v, None)

def back_low(kept, grad):
    return (low(grad),)
low.defvjp(low_keep, low_pass)
low_back.defvjp(back_keep, back_low)
norm_eps = 1e-05

def matmul(left, right):
    return jnp.dot(left, right, precision=lax.Precision.HIGHEST)

def layer_norm(hidden, gain, bias):
    mean = lax.optimization_barrier(jnp.mean(hidden, axis=-1, keepdims=True))
    centered = hidden - mean
    inv_std = lax.rsqrt(lax.optimization_barrier(jnp.mean(centered * centered, axis=-1, keepdims=True)) + norm_eps)
    return centered * inv_std * gain + bias

def attend(packed):
    queries, keyvals, length = packed
    keys = keyvals[:, :HD]
    values = keyvals[:, HD:]
    scores = low_back(jnp.einsum('phd,kd->hpk', queries, keys, precision=lax.Precision.HIGHEST) * (1.0 / math.sqrt(HD)))
    place = jnp.arange(SLOT, dtype=jnp.int32)
    mask = (place[None, :] <= place[:, None]) & (place[None, :] < length)
    probs = jax.nn.softmax(jnp.where(mask[None], scores, -1e+30), axis=-1)
    mixed = jnp.einsum('hpk,kd->phd', low(probs), values, precision=lax.Precision.HIGHEST)
    return low(low_back(mixed.reshape(SLOT, HEADS * HD)))

def forward(tokens, params, lengths, owner_order):
    first_gain, first_bias, w_query, b_query, w_keyval, b_value, w_out, b_out, second_gain, second_bias, w_expand, b_expand, w_contract, b_contract = params
    ordered = jnp.take(tokens, owner_order, axis=0)
    seq_len = jnp.take(lengths, owner_order)
    hidden = ordered.reshape(NSEQ * SLOT, D)
    normed_in = low(layer_norm(hidden, first_gain, first_bias))
    query = low(low_back(matmul(normed_in, w_query) + b_query))
    keyval_bias = jnp.concatenate([jnp.zeros_like(b_value), b_value])
    keyval = low(low_back(matmul(normed_in, w_keyval) + keyval_bias))
    mixed = lax.map(jax.checkpoint(attend), (query.reshape(NSEQ, SLOT, HEADS, HD), keyval.reshape(NSEQ, SLOT, 2 * HD), seq_len))
    branch = low_back(matmul(mixed.reshape(NSEQ * SLOT, D), w_out) + b_out)
    resid = hidden + branch
    normed2_in = low(layer_norm(resid, second_gain, second_bias))
    preact = low_back(matmul(normed2_in, w_expand) + b_expand)
    active = low(jax.nn.gelu(preact, approximate=True))
    output = low_back(matmul(active, w_contract) + b_contract)
    place = jnp.arange(SLOT, dtype=jnp.int32)
    valid = (place[None, :] < seq_len[:, None]).astype(jnp.float32).reshape(NSEQ * SLOT, 1)
    return (valid * (resid + output)).reshape(NSEQ, SLOT, D)

def reference(tokens, cotangent, lengths, owner_order, first_gain, first_bias, w_query, b_query, w_keyval, b_value, w_out, b_out, second_gain, second_bias, w_expand, b_expand, w_contract, b_contract):
    params = tuple((item.astype(jnp.float32) for item in (first_gain, first_bias, w_query, b_query, w_keyval, b_value, w_out, b_out, second_gain, second_bias, w_expand, b_expand, w_contract, b_contract)))

    def apply(inputs, weights):
        return forward(inputs, weights, lengths, owner_order)
    result, pull = jax.vjp(apply, tokens.astype(jnp.float32), params)
    grad_tokens, grads = pull(cotangent.astype(jnp.float32))
    return (result.astype(jnp.bfloat16), grad_tokens, grads[0], grads[1], grads[2], grads[3], grads[4], grads[5], grads[6], grads[7], grads[8], grads[9], grads[10], grads[11], grads[12], grads[13])
```

```python
import functools
import math

import jax
import jax.numpy as jnp
from jax import lax
from jax.experimental import pallas as pl
from jax.experimental.pallas import tpu as pltpu
from jax.sharding import PartitionSpec as P

norm_eps = 1e-05
f32 = jnp.float32
bf16 = jnp.bfloat16
BOTH = ("dp", "seq")


def norm_rows(hidden):
    mean = jnp.mean(hidden, axis=1, keepdims=True)
    centered = hidden - mean
    inv_std = lax.rsqrt(jnp.mean(centered * centered, axis=1, keepdims=True) + norm_eps)
    return (centered * inv_std, inv_std)


def norm_back(grad_normed, normed, inv_std):
    mean_grad = jnp.mean(grad_normed, axis=1, keepdims=True)
    mean_proj = jnp.mean(grad_normed * normed, axis=1, keepdims=True)
    return inv_std * (grad_normed - mean_grad - normed * mean_proj)


def dot(left, right):
    return jnp.dot(left, right, preferred_element_type=f32)


def dot_general(left, right, left_dims, right_dims):
    return lax.dot_general(
        left, right, ((left_dims, right_dims), ((), ())), preferred_element_type=f32
    )


def ring(count):
    return [(i, (i + 1) % count) for i in range(count)]


def ring_gather(piece, count):
    me = lax.axis_index("dp")
    whole = jnp.zeros((count,) + piece.shape, piece.dtype)
    whole = lax.dynamic_update_index_in_dim(whole, piece, me, 0)
    moving = piece
    for step in range(1, count):
        moving = lax.ppermute(moving, "dp", ring(count))
        whole = lax.dynamic_update_index_in_dim(whole, moving, (me - step) % count, 0)
    return whole


def ring_scatter(parts, count):
    me = lax.axis_index("dp")
    moving = None
    for step in range(count):
        mine = lax.dynamic_index_in_dim(parts, (me - 1 - step) % count, 0, keepdims=False)
        mine = mine.astype(f32)
        total = mine if moving is None else mine + moving.astype(f32)
        if step < count - 1:
            moving = lax.ppermute(total.astype(bf16), "dp", ring(count))
    return total


def block_probs(query, key, limit, scale):
    raw = dot_general(query, key, (1,), (1,)) * scale
    place = lax.broadcasted_iota(jnp.int32, raw.shape, 1)
    masked = jnp.where(place <= limit, raw, -1e30)
    top = jnp.max(masked, axis=1, keepdims=True)
    unnormed = jnp.exp(masked - top)
    return unnormed / jnp.sum(unnormed, axis=1, keepdims=True)


def row_limit(first, rows, length):
    place = first + lax.broadcasted_iota(jnp.int32, (rows, 1), 0)
    return jnp.minimum(place, length - 1)


def attend_kernel(rows, scale, lengths_ref, query_ref, keyval_ref, mixed_ref):
    length = lengths_ref[pl.program_id(0)]
    blocks, one, block, size = query_ref.shape
    total = blocks * block
    step = rows // block
    for at in range(total // rows):
        span = (at + 1) * rows
        query = query_ref[at * step : (at + 1) * step].reshape(rows, size)
        keyval = keyval_ref[: (at + 1) * step].reshape(span, 2 * size)
        probs = block_probs(query, keyval[:, :size], row_limit(at * rows, rows, length), scale)
        mixed = dot(probs.astype(bf16), keyval[:, size:])
        mixed_ref[at * step : (at + 1) * step] = mixed.astype(bf16).reshape(step, 1, block, size)


def attend_back_kernel(
    rows, scale, lengths_ref, query_ref, keyval_ref, grad_ref, grad_query_ref, grad_keyval_ref, sums
):
    length = lengths_ref[pl.program_id(0)]
    head = pl.program_id(1)
    blocks, one, block, size = query_ref.shape
    total = blocks * block
    step = rows // block

    @pl.when(head == 0)
    def _():
        sums[...] = jnp.zeros_like(sums)

    for at in range(total // rows):
        span = (at + 1) * rows
        query = query_ref[at * step : (at + 1) * step].reshape(rows, size)
        grad = grad_ref[at * step : (at + 1) * step].reshape(rows, size)
        keyval = keyval_ref[: (at + 1) * step].reshape(span, 2 * size)
        probs = block_probs(query, keyval[:, :size], row_limit(at * rows, rows, length), scale)
        grad_probs = dot_general(grad, keyval[:, size:], (1,), (1,))
        inner = jnp.sum(probs * grad_probs, axis=1, keepdims=True)
        grad_scores = (probs * (grad_probs - inner)).astype(bf16)
        grad_query = (dot(grad_scores, keyval[:, :size]) * scale).astype(bf16)
        grad_query_ref[at * step : (at + 1) * step] = grad_query.reshape(step, 1, block, size)
        sums[:span, :size] += dot_general(grad_scores, query, (0,), (0,)) * scale
        sums[:span, size:] += dot_general(probs.astype(bf16), grad, (0,), (0,))

    @pl.when(head == pl.num_programs(1) - 1)
    def _():
        grad_keyval_ref[...] = sums[...].astype(bf16).reshape(grad_keyval_ref.shape)


def attention_calls(shape, head_size, rows):
    blocks, micro, block, width = shape
    heads = width // head_size
    scale = 1.0 / math.sqrt(head_size)
    head_spec = pl.BlockSpec((blocks, 1, block, head_size), lambda m, h, n: (0, m, 0, h))
    keyval_spec = pl.BlockSpec((blocks, 1, block, 2 * head_size), lambda m, h, n: (0, m, 0, 0))
    area = micro * heads * (blocks * block) ** 2 * head_size
    size = blocks * micro * block * (width + 2 * head_size) * 2
    head_out = jax.ShapeDtypeStruct(shape, bf16)
    keyval_out = jax.ShapeDtypeStruct((blocks, micro, block, 2 * head_size), bf16)
    params = pltpu.CompilerParams(vmem_limit_bytes=56 * 2**20)
    forward = pl.pallas_call(
        functools.partial(attend_kernel, rows, scale),
        out_shape=head_out,
        grid_spec=pltpu.PrefetchScalarGridSpec(
            num_scalar_prefetch=1,
            grid=(micro, heads),
            in_specs=[head_spec, keyval_spec],
            out_specs=head_spec,
        ),
        compiler_params=params,
        cost_estimate=pl.CostEstimate(
            flops=4 * area, bytes_accessed=2 * size, transcendentals=area // head_size
        ),
        name="attend",
    )
    backward = pl.pallas_call(
        functools.partial(attend_back_kernel, rows, scale),
        out_shape=(head_out, keyval_out),
        grid_spec=pltpu.PrefetchScalarGridSpec(
            num_scalar_prefetch=1,
            grid=(micro, heads),
            in_specs=[head_spec, keyval_spec, head_spec],
            out_specs=[head_spec, keyval_spec],
            scratch_shapes=[pltpu.VMEM((blocks * block, 2 * head_size), f32)],
        ),
        compiler_params=params,
        cost_estimate=pl.CostEstimate(
            flops=10 * area, bytes_accessed=4 * size, transcendentals=area // head_size
        ),
        name="attend_back",
    )
    return forward, backward


def gelu_parts(value):
    root = math.sqrt(2.0 / math.pi)
    square = value * value
    bent = jnp.tanh(root * value * (1.0 + 0.044715 * square))
    active = 0.5 * value * (1.0 + bent)
    slope = 0.5 * (1.0 + bent) + 0.5 * value * (1.0 - bent * bent) * root * (
        1.0 + 3.0 * 0.044715 * square
    )
    return active, slope


def shards(
    parts,
    ranks,
    tokens,
    cotangent,
    lengths,
    owner_order,
    first_gain,
    first_bias,
    w_query,
    b_query,
    w_keyval,
    b_value,
    w_out,
    b_out,
    second_gain,
    second_bias,
    w_expand,
    b_expand,
    w_contract,
    b_contract,
):
    micro, block, width = tokens.shape
    head_size = w_keyval.shape[1] // 2
    every = parts * ranks
    rows = micro * block
    all_rows = ranks * rows
    head_cols = width // ranks
    strip = w_query.shape[0]
    hidden_strip = w_contract.shape[0]
    hidden_cols = parts * hidden_strip
    owner = lax.axis_index("dp")
    rank = lax.axis_index("seq")
    seq_ids = jnp.arange(lengths.shape[0], dtype=jnp.int32)
    own_length = lax.dynamic_slice_in_dim(lengths, owner * micro, micro)
    place = rank * block + jnp.arange(block, dtype=jnp.int32)
    valid = (place[None, :] < own_length[:, None]).astype(f32).reshape(rows, 1)

    tokens_all = lax.all_gather(tokens.reshape(rows, width), "seq", axis=0, tiled=True)
    smalls = [
        first_gain,
        first_bias,
        b_query,
        b_out,
        second_gain,
        second_bias,
        b_contract,
        b_expand,
        b_value,
    ]
    lengths_of = [item.shape[0] for item in smalls]
    pad = -sum(lengths_of) % (2 * head_size)
    packed = jnp.concatenate(smalls + [jnp.zeros((pad,), bf16)]).reshape(-1, 2 * head_size)
    packed = jnp.concatenate([w_keyval, packed], axis=0)
    packed = lax.all_gather(packed, BOTH, axis=0, tiled=False)
    keyval_weight = packed[:, :strip].reshape(width, 2 * head_size)
    packed = packed[:, strip:].reshape(every, -1)
    whole = []
    at = 0
    for count in lengths_of:
        whole.append(packed[:, at : at + count].astype(f32))
        at += count
    gain_one, bias_one, query_bias, out_bias, gain_two, bias_two, contract_bias = [
        item.reshape(1, width) for item in whole[:7]
    ]
    expand_bias = lax.dynamic_index_in_dim(
        whole[7].reshape(parts, ranks, hidden_strip), rank, 1, keepdims=False
    ).reshape(1, hidden_cols)
    value_bias = whole[8].reshape(1, head_size)
    query_bias = lax.dynamic_slice_in_dim(query_bias, rank * head_cols, head_cols, axis=1)
    keyval_bias = jnp.concatenate([jnp.zeros_like(value_bias), value_bias], axis=1)

    sent = jnp.concatenate(
        [
            w_query.reshape(strip, ranks, head_cols).transpose(1, 0, 2),
            w_expand.reshape(strip, parts, ranks, hidden_strip)
            .transpose(2, 0, 1, 3)
            .reshape(ranks, strip, hidden_cols),
        ],
        axis=2,
    )
    sent = lax.all_to_all(sent, "seq", 0, 0).reshape(ranks * strip, head_cols + hidden_cols)
    query_weight = ring_gather(sent[:, :head_cols], parts).reshape(width, head_cols)
    moved = [(f, (f % parts) * ranks + f // parts) for f in range(every)]
    out_weight = ring_gather(lax.ppermute(w_out, BOTH, moved), parts)
    out_weight = lax.all_gather(out_weight.reshape(head_cols, width), "seq", axis=0, tiled=True)
    cotangent_all = ring_gather(cotangent, parts).reshape(-1, block, width)
    expand_weight = ring_gather(sent[:, head_cols:], parts).reshape(width, hidden_cols)
    contract_weight = ring_gather(w_contract, parts).reshape(hidden_cols, width)

    mine = owner * micro + jnp.arange(micro, dtype=jnp.int32)
    slots = jnp.sum(jnp.where(owner_order[None, :] == mine[:, None], seq_ids[None, :], 0), axis=1)
    grad_y = jnp.stack(
        [lax.dynamic_index_in_dim(cotangent_all, slots[i], 0, keepdims=False) for i in range(micro)]
    )
    grad_y = grad_y.reshape(rows, width).astype(f32) * valid
    grad_m = grad_y.astype(bf16)
    grad_m_all = lax.all_gather(grad_m, "seq", axis=0, tiled=True)

    head_shape = (ranks, micro, block, head_cols)
    attend, attend_back = attention_calls(head_shape, head_size, 2 * block)
    normed_all, unused_std = norm_rows(tokens_all.astype(f32))
    normed_in_all = (normed_all * gain_one + bias_one).astype(bf16)
    query = (dot(normed_in_all, query_weight) + query_bias).astype(bf16)
    keyval = (dot(normed_in_all, keyval_weight) + keyval_bias).astype(bf16)
    query = query.reshape(head_shape)
    keyval = keyval.reshape(ranks, micro, block, 2 * head_size)
    mixed = attend(own_length, query, keyval)
    mixed_rows = lax.all_to_all(mixed, "seq", 0, 0).reshape(ranks, rows, head_cols)
    mixed_rows = mixed_rows.transpose(1, 0, 2).reshape(rows, width)

    hidden = tokens.reshape(rows, width).astype(f32)
    resid = hidden + dot(mixed_rows, out_weight) + out_bias
    normed2, inv_std2 = norm_rows(resid)
    normed2_in = (normed2 * gain_two + bias_two).astype(bf16)
    normed2_all = lax.all_gather(normed2_in, "seq", axis=0, tiled=True)

    preact = dot(normed2_all, expand_weight) + expand_bias
    active, slope = gelu_parts(preact)
    active = active.astype(bf16)
    grad_active = dot_general(grad_m_all, contract_weight, (1,), (1,))
    grad_pre = (grad_active * slope).astype(bf16)
    grad_c = dot_general(grad_pre, expand_weight, (1,), (1,)).astype(bf16)
    grad_c = lax.psum_scatter(grad_c, "seq", scatter_dimension=0, tiled=True).astype(f32)
    output = dot(active, contract_weight).astype(bf16)
    output = lax.psum_scatter(output, "seq", scatter_dimension=0, tiled=True).astype(f32)
    result = (valid * (resid + output + contract_bias)).astype(bf16)
    result_all = ring_gather(result.reshape(micro, block, width), parts).reshape(-1, block, width)
    wanted = lax.dynamic_slice_in_dim(owner_order, owner * micro, micro)
    result = jnp.stack(
        [lax.dynamic_index_in_dim(result_all, wanted[i], 0, keepdims=False) for i in range(micro)]
    )
    grad_contract = dot_general(active, grad_m_all, (0,), (0,))
    grad_contract = ring_scatter(grad_contract.reshape(parts, hidden_strip, width), parts)
    grad_expand = dot_general(normed2_all, grad_pre, (0,), (0,))
    grad_expand = ring_scatter(
        grad_expand.reshape(parts, ranks * strip, hidden_cols), parts
    ).astype(bf16)
    grad_expand = lax.all_to_all(grad_expand.reshape(ranks, strip, hidden_cols), "seq", 0, 0)
    grad_expand = (
        grad_expand.reshape(ranks, strip, parts, hidden_strip)
        .transpose(1, 2, 0, 3)
        .reshape(strip, every * hidden_strip)
        .astype(f32)
    )

    grad_resid = grad_y + norm_back(grad_c * gain_two, normed2, inv_std2)
    grad_branch = grad_resid.astype(bf16)
    grad_mixed = dot_general(grad_branch, out_weight, (1,), (1,)).astype(bf16)
    grad_mixed = grad_mixed.reshape(rows, ranks, head_cols).transpose(1, 0, 2)
    grad_mixed = lax.all_to_all(grad_mixed, "seq", 0, 0).reshape(head_shape)
    grad_query, grad_keyval = attend_back(own_length, query, keyval, grad_mixed)
    grad_branch_all = lax.all_gather(grad_branch, "seq", axis=0, tiled=True)
    grad_out = dot_general(mixed.reshape(all_rows, head_cols), grad_branch_all, (0,), (0,))
    grad_out = ring_scatter(grad_out.reshape(parts, head_cols // parts, width), parts)
    back = [(d * ranks + s, s * parts + d) for d in range(parts) for s in range(ranks)]
    grad_out = lax.ppermute(grad_out.astype(bf16), BOTH, back).astype(f32)

    both = jnp.concatenate([grad_query, grad_keyval], axis=3).reshape(all_rows, -1)
    grad_in_weight = dot_general(normed_in_all, both, (0,), (0,))
    grad_in_weight = ring_scatter(
        grad_in_weight.reshape(parts, ranks * strip, both.shape[1]), parts
    ).astype(bf16)
    grad_in_weight = lax.all_to_all(
        grad_in_weight.reshape(ranks, strip, both.shape[1]), "seq", 0, 0
    )
    grad_query_weight = (
        grad_in_weight[:, :, :head_cols].transpose(1, 0, 2).reshape(strip, width).astype(f32)
    )
    grad_keyval_weight = jnp.sum(grad_in_weight[:, :, head_cols:].astype(f32), axis=0)

    query_weight_all = lax.all_gather(query_weight, "seq", axis=0, tiled=False)
    both = lax.all_to_all(both.reshape(ranks, rows, -1), "seq", 0, 0)
    grad_query_rows = both[:, :, :head_cols]
    grad_keyval_rows = jnp.sum(both[:, :, head_cols:].astype(f32), axis=0).astype(bf16)
    grad_in = dot_general(grad_query_rows, query_weight_all, (0, 2), (0, 2))
    grad_in = grad_in + dot_general(grad_keyval_rows, keyval_weight, (1,), (1,))
    normed, inv_std = norm_rows(hidden)
    grad_tokens = grad_resid + norm_back(grad_in * gain_one, normed, inv_std)

    def spread(values):
        return values.reshape(every, -1)

    def column_sum(values):
        return jnp.sum(values.astype(f32), axis=0)

    expand_sum = column_sum(grad_pre).reshape(parts, 1, hidden_strip)
    here = jnp.arange(ranks, dtype=jnp.int32)[None, :, None] == rank
    expand_sum = jnp.where(here, expand_sum, 0.0).reshape(every, hidden_strip)
    sums = jnp.concatenate(
        [
            spread(column_sum(grad_in * normed)),
            spread(column_sum(grad_in)),
            spread(column_sum(grad_query_rows.transpose(1, 0, 2).reshape(rows, width))),
            spread(column_sum(grad_branch)),
            spread(column_sum(grad_c * normed2)),
            spread(column_sum(grad_c)),
            spread(column_sum(grad_m)),
            expand_sum,
            spread(column_sum(grad_keyval_rows)[head_size:]),
        ],
        axis=1,
    )
    sums = lax.psum_scatter(sums, BOTH, scatter_dimension=0, tiled=True).reshape(-1)
    small_grads = []
    at = 0
    for count in lengths_of:
        small_grads.append(sums[at : at + count])
        at += count
    return (
        result,
        grad_tokens.reshape(micro, block, width),
        small_grads[0],
        small_grads[1],
        grad_query_weight,
        small_grads[2],
        grad_keyval_weight,
        small_grads[8],
        grad_out,
        small_grads[3],
        small_grads[4],
        small_grads[5],
        grad_expand,
        small_grads[7],
        grad_contract,
        small_grads[6],
    )


def solution(mesh):
    split = P(BOTH)
    rows = P(BOTH, None)
    moved = P("dp", "seq", None)
    return jax.shard_map(
        functools.partial(shards, mesh.shape["dp"], mesh.shape["seq"]),
        mesh=mesh,
        in_specs=(
            moved,
            moved,
            P(),
            P(),
            split,
            split,
            rows,
            split,
            rows,
            split,
            rows,
            split,
            split,
            split,
            rows,
            split,
            rows,
            split,
        ),
        out_specs=(
            moved,
            moved,
            split,
            split,
            rows,
            split,
            rows,
            split,
            rows,
            split,
            split,
            split,
            rows,
            split,
            rows,
            split,
        ),
        check_vma=False,
    )
```

```python
import functools
import math

import jax
import jax.numpy as jnp
from jax import lax
from jax.experimental import pallas as pl
from jax.experimental.pallas import tpu as pltpu
from jax.sharding import PartitionSpec as P

norm_eps = 1e-05
f32 = jnp.float32
bf16 = jnp.bfloat16
BOTH = ("dp", "seq")


def norm_rows(hidden):
    mean = jnp.mean(hidden, axis=1, keepdims=True)
    centered = hidden - mean
    inv_std = lax.rsqrt(jnp.mean(centered * centered, axis=1, keepdims=True) + norm_eps)
    return (centered * inv_std, inv_std)


def norm_back(grad_normed, normed, inv_std):
    mean_grad = jnp.mean(grad_normed, axis=1, keepdims=True)
    mean_proj = jnp.mean(grad_normed * normed, axis=1, keepdims=True)
    return inv_std * (grad_normed - mean_grad - normed * mean_proj)


def dot(left, right):
    return jnp.dot(left, right, preferred_element_type=f32)


def dot_general(left, right, left_dims, right_dims):
    return lax.dot_general(
        left, right, ((left_dims, right_dims), ((), ())), preferred_element_type=f32
    )


def shift(count, by):
    return [(i, (i + by) % count) for i in range(count)]


def gather_parts(piece, count):
    me = lax.axis_index("dp")
    whole = jnp.zeros((count,) + piece.shape, piece.dtype)
    whole = lax.dynamic_update_index_in_dim(whole, piece, me, 0)
    for by in range(1, count):
        moved = lax.ppermute(piece, "dp", shift(count, by))
        whole = lax.dynamic_update_index_in_dim(whole, moved, (me - by) % count, 0)
    return whole


def ring_pieces(piece, count):
    pieces = [piece]
    for step in range(1, count):
        pieces.append(lax.ppermute(pieces[-1], "dp", shift(count, 1)))
    return pieces


def exchange_parts(pieces, count):
    me = lax.axis_index("dp")
    own = lax.dynamic_index_in_dim(pieces, me, 0, keepdims=False)
    whole = lax.dynamic_update_index_in_dim(jnp.zeros_like(pieces), own, me, 0)
    for by in range(1, count):
        piece = lax.dynamic_index_in_dim(pieces, (me + by) % count, 0, keepdims=False)
        moved = lax.ppermute(piece, "dp", shift(count, by))
        whole = lax.dynamic_update_index_in_dim(whole, moved, (me - by) % count, 0)
    return whole


def ring_sum(part_for, count):
    moving = None
    for step in range(count):
        total = part_for((1 + step) % count)
        if moving is not None:
            total = total + moving.astype(f32)
        if step < count - 1:
            moving = lax.ppermute(total.astype(bf16), "dp", shift(count, 1))
    return total


def ring_scatter(parts, count):
    me = lax.axis_index("dp")

    def part_for(by):
        return lax.dynamic_index_in_dim(parts, (me - by) % count, 0, keepdims=False).astype(f32)

    return ring_sum(part_for, count)


def halve(values, axis, bit, rank, count):
    mine = (rank >> bit) & 1
    keep = lax.dynamic_index_in_dim(values, mine, axis, keepdims=False)
    give = lax.dynamic_index_in_dim(values, 1 - mine, axis, keepdims=False)
    moved = lax.ppermute(give.astype(bf16), "seq", [(i, i ^ (1 << bit)) for i in range(count)])
    return keep.astype(f32) + moved.astype(f32)


def rank_scatter(values, count):
    rank = lax.axis_index("seq")
    bits = count.bit_length() - 1
    outer, unused, length, width = values.shape
    halves = values.reshape((outer,) + (2,) * bits + (2, length // 2, width))
    halves = halve(halves, bits, 0, rank, count).astype(bf16)
    done = []
    for at in range(2):
        half = lax.index_in_dim(halves, at, bits, keepdims=False)
        left = list(range(bits - 1, 0, -1))
        order = left[::-1] if at == 0 else left[:]
        for bit in order:
            half = halve(half, 1 + left.index(bit), bit, rank, count)
            left.remove(bit)
            if left:
                half = half.astype(bf16)
        done.append(half)
    return jnp.concatenate(done, axis=1)


def block_probs(query, key, limit, scale):
    raw = dot_general(query, key, (1,), (1,)) * scale
    place = lax.broadcasted_iota(jnp.int32, raw.shape, 1)
    masked = jnp.where(place <= limit, raw, -1e30)
    top = jnp.max(masked, axis=1, keepdims=True)
    unnormed = jnp.exp(masked - top)
    return unnormed / jnp.sum(unnormed, axis=1, keepdims=True)


def row_limit(first, rows, length):
    place = first + lax.broadcasted_iota(jnp.int32, (rows, 1), 0)
    return jnp.minimum(place, length - 1)


def attend_kernel(rows, scale, lengths_ref, query_ref, keyval_ref, mixed_ref):
    length = lengths_ref[pl.program_id(0)]
    blocks, one, block, size = query_ref.shape
    total = blocks * block
    step = rows // block
    for at in range(total // rows):
        span = (at + 1) * rows
        query = query_ref[at * step : (at + 1) * step].reshape(rows, size)
        keyval = keyval_ref[: (at + 1) * step].reshape(span, 2 * size)
        probs = block_probs(query, keyval[:, :size], row_limit(at * rows, rows, length), scale)
        mixed = dot(probs.astype(bf16), keyval[:, size:])
        mixed_ref[at * step : (at + 1) * step] = mixed.astype(bf16).reshape(step, 1, block, size)


def attend_back_kernel(
    rows, scale, lengths_ref, query_ref, keyval_ref, grad_ref, grad_query_ref, grad_keyval_ref, sums
):
    length = lengths_ref[pl.program_id(0)]
    head = pl.program_id(1)
    blocks, one, block, size = query_ref.shape
    total = blocks * block
    step = rows // block

    @pl.when(head == 0)
    def _():
        sums[...] = jnp.zeros_like(sums)

    for at in range(total // rows):
        span = (at + 1) * rows
        query = query_ref[at * step : (at + 1) * step].reshape(rows, size)
        grad = grad_ref[at * step : (at + 1) * step].reshape(rows, size)
        keyval = keyval_ref[: (at + 1) * step].reshape(span, 2 * size)
        probs = block_probs(query, keyval[:, :size], row_limit(at * rows, rows, length), scale)
        grad_probs = dot_general(grad, keyval[:, size:], (1,), (1,))
        inner = jnp.sum(probs * grad_probs, axis=1, keepdims=True)
        grad_scores = (probs * (grad_probs - inner)).astype(bf16)
        grad_query = (dot(grad_scores, keyval[:, :size]) * scale).astype(bf16)
        grad_query_ref[at * step : (at + 1) * step] = grad_query.reshape(step, 1, block, size)
        sums[:span, :size] += dot_general(grad_scores, query, (0,), (0,)) * scale
        sums[:span, size:] += dot_general(probs.astype(bf16), grad, (0,), (0,))

    @pl.when(head == pl.num_programs(1) - 1)
    def _():
        grad_keyval_ref[...] = sums[...].astype(bf16).reshape(grad_keyval_ref.shape)


def attention_calls(shape, head_size, rows):
    blocks, micro, block, width = shape
    heads = width // head_size
    scale = 1.0 / math.sqrt(head_size)
    head_spec = pl.BlockSpec((blocks, 1, block, head_size), lambda m, h, n: (0, m, 0, h))
    keyval_spec = pl.BlockSpec((blocks, 1, block, 2 * head_size), lambda m, h, n: (0, m, 0, 0))
    area = micro * heads * (blocks * block) ** 2 * head_size
    size = blocks * micro * block * (width + 2 * head_size) * 2
    head_out = jax.ShapeDtypeStruct(shape, bf16)
    keyval_out = jax.ShapeDtypeStruct((blocks, micro, block, 2 * head_size), bf16)
    params = pltpu.CompilerParams(vmem_limit_bytes=56 * 2**20)
    forward = pl.pallas_call(
        functools.partial(attend_kernel, rows, scale),
        out_shape=head_out,
        grid_spec=pltpu.PrefetchScalarGridSpec(
            num_scalar_prefetch=1,
            grid=(micro, heads),
            in_specs=[head_spec, keyval_spec],
            out_specs=head_spec,
        ),
        compiler_params=params,
        cost_estimate=pl.CostEstimate(
            flops=4 * area, bytes_accessed=2 * size, transcendentals=area // head_size
        ),
        name="attend",
    )
    backward = pl.pallas_call(
        functools.partial(attend_back_kernel, rows, scale),
        out_shape=(head_out, keyval_out),
        grid_spec=pltpu.PrefetchScalarGridSpec(
            num_scalar_prefetch=1,
            grid=(micro, heads),
            in_specs=[head_spec, keyval_spec, head_spec],
            out_specs=[head_spec, keyval_spec],
            scratch_shapes=[pltpu.VMEM((blocks * block, 2 * head_size), f32)],
        ),
        compiler_params=params,
        cost_estimate=pl.CostEstimate(
            flops=10 * area, bytes_accessed=4 * size, transcendentals=area // head_size
        ),
        name="attend_back",
    )
    return forward, backward


def gelu_parts(value):
    root = math.sqrt(2.0 / math.pi)
    square = value * value
    bent = jnp.tanh(root * value * (1.0 + 0.044715 * square))
    active = 0.5 * value * (1.0 + bent)
    slope = 0.5 * (1.0 + bent) + 0.5 * value * (1.0 - bent * bent) * root * (
        1.0 + 3.0 * 0.044715 * square
    )
    return active, slope


def shards(
    parts,
    ranks,
    tokens,
    cotangent,
    lengths,
    owner_order,
    first_gain,
    first_bias,
    w_query,
    b_query,
    w_keyval,
    b_value,
    w_out,
    b_out,
    second_gain,
    second_bias,
    w_expand,
    b_expand,
    w_contract,
    b_contract,
):
    micro, block, width = tokens.shape
    head_size = w_keyval.shape[1] // 2
    every = parts * ranks
    rows = micro * block
    all_rows = ranks * rows
    head_cols = width // ranks
    strip = w_query.shape[0]
    hidden_strip = w_contract.shape[0]
    hidden_cols = ranks * hidden_strip
    owner = lax.axis_index("dp")
    rank = lax.axis_index("seq")
    seq_ids = jnp.arange(lengths.shape[0], dtype=jnp.int32)
    own_length = lax.dynamic_slice_in_dim(lengths, owner * micro, micro)
    place = rank * block + jnp.arange(block, dtype=jnp.int32)

    tokens_all = lax.all_gather(tokens.reshape(rows, width), "seq", axis=0, tiled=True)
    smalls = [
        first_gain,
        first_bias,
        b_query,
        b_out,
        second_gain,
        second_bias,
        b_contract,
        b_expand,
        b_value,
    ]
    lengths_of = [item.shape[0] for item in smalls]
    pad = -sum(lengths_of) % (16 * head_size)
    packed = jnp.concatenate(smalls + [jnp.zeros((pad,), bf16)]).reshape(-1, 2 * head_size)
    packed = jnp.concatenate([w_keyval, packed], axis=0)
    packed = jnp.broadcast_to(packed[None], (every,) + packed.shape)
    packed = lax.all_to_all(packed, BOTH, 0, 0)
    keyval_weight = packed[:, :strip].reshape(width, 2 * head_size)
    packed = packed[:, strip:].reshape(every, -1)
    whole = []
    at = 0
    for count in lengths_of:
        whole.append(packed[:, at : at + count].astype(f32))
        at += count
    gain_one, bias_one, query_bias, out_bias, gain_two, bias_two, contract_bias = [
        item.reshape(1, width) for item in whole[:7]
    ]
    expand_bias = lax.dynamic_slice_in_dim(whole[7], owner * ranks, ranks)
    expand_bias = expand_bias.reshape(1, hidden_cols)
    value_bias = whole[8].reshape(1, head_size)
    query_bias = lax.dynamic_slice_in_dim(query_bias, rank * head_cols, head_cols, axis=1)
    keyval_bias = jnp.concatenate([jnp.zeros_like(value_bias), value_bias], axis=1)

    sent = w_query.reshape(strip, ranks, head_cols).transpose(1, 0, 2)
    sent = lax.all_to_all(sent, "seq", 0, 0).reshape(ranks * strip, head_cols)
    query_weight = gather_parts(sent, parts).reshape(width, head_cols)
    moved = [(f, (f % parts) * ranks + f // parts) for f in range(every)]
    out_weight = gather_parts(lax.ppermute(w_out, BOTH, moved), parts)
    out_weight = lax.all_gather(out_weight.reshape(head_cols, width), "seq", axis=0, tiled=True)
    sent = w_expand.reshape(strip, parts, hidden_cols).transpose(1, 0, 2)
    sent = exchange_parts(sent, parts).reshape(parts * strip, hidden_cols)
    expand_weight = lax.all_gather(sent, "seq", axis=0, tiled=False)
    expand_weight = (
        expand_weight.reshape(ranks, parts, strip, hidden_cols)
        .transpose(1, 0, 2, 3)
        .reshape(width, hidden_cols)
    )
    contract_weight = lax.all_gather(w_contract, "seq", axis=0, tiled=True)

    cotangents = jnp.stack(ring_pieces(cotangent, parts)).reshape(-1, block, width)
    slot_of = jnp.sum(
        jnp.where(owner_order[None, :] == seq_ids[:, None], seq_ids[None, :], 0), axis=1
    )

    def grad_of(behind):
        taken = []
        for i in range(micro):
            seq = ((owner - behind) % parts) * micro + i
            slot = slot_of[seq]
            at = ((owner - slot // micro) % parts) * micro + slot % micro
            piece = lax.dynamic_index_in_dim(cotangents, at, 0, keepdims=False)
            inside = (place < lengths[seq])[:, None]
            taken.append(jnp.where(inside, piece, jnp.zeros_like(piece)))
        return jnp.concatenate(taken, axis=0)

    grad_ms = [grad_of(behind) for behind in range(parts)]
    grad_y = grad_ms[0].astype(f32)

    head_shape = (ranks, micro, block, head_cols)
    attend, attend_back = attention_calls(head_shape, head_size, 2 * block)
    normed_all, unused_std = norm_rows(tokens_all.astype(f32))
    normed_in_all = (normed_all * gain_one + bias_one).astype(bf16)
    query = (dot(normed_in_all, query_weight) + query_bias).astype(bf16)
    keyval = (dot(normed_in_all, keyval_weight) + keyval_bias).astype(bf16)
    query = query.reshape(head_shape)
    keyval = keyval.reshape(ranks, micro, block, 2 * head_size)
    mixed = attend(own_length, query, keyval)
    mixed_rows = lax.all_to_all(mixed, "seq", 0, 0).reshape(ranks, rows, head_cols)
    mixed_rows = mixed_rows.transpose(1, 0, 2).reshape(rows, width)

    hidden = tokens.reshape(rows, width).astype(f32)
    resid = hidden + dot(mixed_rows, out_weight) + out_bias
    normed2, inv_std2 = norm_rows(resid)
    normed2_in = (normed2 * gain_two + bias_two).astype(bf16)

    normed2_ins = ring_pieces(normed2_in, parts)
    actives = [None] * parts
    grad_pres = [None] * parts

    def grad_c_for(behind):
        preact = dot(normed2_ins[behind], expand_weight) + expand_bias
        active, slope = gelu_parts(preact)
        actives[behind] = active.astype(bf16)
        grad_active = dot_general(grad_ms[behind], contract_weight, (1,), (1,))
        grad_pres[behind] = (grad_active * slope).astype(bf16)
        return dot_general(grad_pres[behind], expand_weight, (1,), (1,))

    grad_c = ring_sum(grad_c_for, parts)
    outputs = jnp.stack([dot(active, contract_weight).astype(bf16) for active in actives])
    outputs = outputs.reshape(parts * micro, block, width)
    resid_rows = resid.reshape(micro, block, width)

    def output_for(behind):
        taken = []
        for i in range(micro):
            seq = owner_order[((owner - behind) % parts) * micro + i]
            source = (owner - seq // micro) % parts
            piece = lax.dynamic_index_in_dim(
                outputs, source * micro + seq % micro, 0, keepdims=False
            )
            own = lax.dynamic_index_in_dim(resid_rows, seq % micro, 0, keepdims=False)
            taken.append(piece.astype(f32) + jnp.where(source == 0, own, 0.0))
        return jnp.stack(taken)

    result = ring_sum(output_for, parts)
    held = lax.dynamic_slice_in_dim(owner_order, owner * micro, micro)
    held_length = jnp.sum(jnp.where(held[:, None] == seq_ids[None, :], lengths[None, :], 0), axis=1)
    held_valid = (place[None, :] < held_length[:, None])[:, :, None]
    result = jnp.where(held_valid, result + contract_bias, 0.0).astype(bf16)

    active_all = jnp.concatenate(actives, axis=0)
    grad_pre_all = jnp.concatenate(grad_pres, axis=0)
    grad_m_all = jnp.concatenate(grad_ms, axis=0)
    normed2_all = jnp.concatenate(normed2_ins, axis=0)
    grad_contract = dot_general(active_all, grad_m_all, (0,), (0,)).astype(bf16)
    grad_contract = rank_scatter(grad_contract.reshape(1, ranks, hidden_strip, width), ranks)
    grad_contract = grad_contract.reshape(hidden_strip, width)
    grad_expand = dot_general(normed2_all, grad_pre_all, (0,), (0,)).astype(bf16)
    grad_expand = rank_scatter(grad_expand.reshape(parts, ranks, strip, hidden_cols), ranks)
    grad_expand = exchange_parts(grad_expand.astype(bf16), parts)
    grad_expand = grad_expand.transpose(1, 0, 2).reshape(strip, -1).astype(f32)

    grad_resid = grad_y + norm_back(grad_c * gain_two, normed2, inv_std2)
    grad_branch = grad_resid.astype(bf16)
    grad_mixed = dot_general(grad_branch, out_weight, (1,), (1,)).astype(bf16)
    grad_mixed = grad_mixed.reshape(rows, ranks, head_cols).transpose(1, 0, 2)
    grad_mixed = lax.all_to_all(grad_mixed, "seq", 0, 0).reshape(head_shape)
    grad_query, grad_keyval = attend_back(own_length, query, keyval, grad_mixed)
    grad_branch_all = lax.all_gather(grad_branch, "seq", axis=0, tiled=True)
    grad_out = dot_general(mixed.reshape(all_rows, head_cols), grad_branch_all, (0,), (0,))
    grad_out = ring_scatter(grad_out.reshape(parts, head_cols // parts, width), parts)
    back = [(d * ranks + s, s * parts + d) for d in range(parts) for s in range(ranks)]
    grad_out = lax.ppermute(grad_out.astype(bf16), BOTH, back).astype(f32)

    both = jnp.concatenate([grad_query, grad_keyval], axis=3).reshape(all_rows, -1)
    grad_in_weight = dot_general(normed_in_all, both, (0,), (0,))
    grad_in_weight = ring_scatter(
        grad_in_weight.reshape(parts, ranks * strip, both.shape[1]), parts
    ).astype(bf16)
    grad_in_weight = lax.all_to_all(
        grad_in_weight.reshape(ranks, strip, both.shape[1]), "seq", 0, 0
    )
    grad_query_weight = (
        grad_in_weight[:, :, :head_cols].transpose(1, 0, 2).reshape(strip, width).astype(f32)
    )
    grad_keyval_weight = jnp.sum(grad_in_weight[:, :, head_cols:].astype(f32), axis=0)

    query_weight_all = lax.all_gather(query_weight.T, "seq", axis=0, tiled=True)
    both = lax.all_to_all(both.reshape(ranks, rows, -1), "seq", 0, 0)
    grad_query_rows = both[:, :, :head_cols].transpose(1, 0, 2).reshape(rows, width)
    grad_keyval_rows = jnp.sum(both[:, :, head_cols:].astype(f32), axis=0).astype(bf16)
    grad_in = dot(grad_query_rows, query_weight_all)
    grad_in = grad_in + dot_general(grad_keyval_rows, keyval_weight, (1,), (1,))
    normed, inv_std = norm_rows(hidden)
    grad_tokens = grad_resid + norm_back(grad_in * gain_one, normed, inv_std)

    def spread(values):
        return values.reshape(every, -1)

    def column_sum(values):
        return jnp.sum(values.astype(f32), axis=0)

    expand_sum = column_sum(grad_pre_all).reshape(1, ranks, hidden_strip)
    here = jnp.arange(parts, dtype=jnp.int32)[:, None, None] == owner
    expand_sum = jnp.where(here, expand_sum, 0.0).reshape(every, hidden_strip)
    sums = jnp.concatenate(
        [
            spread(column_sum(grad_in * normed)),
            spread(column_sum(grad_in)),
            spread(column_sum(grad_query_rows)),
            spread(column_sum(grad_branch)),
            spread(column_sum(grad_c * normed2)),
            spread(column_sum(grad_c)),
            spread(column_sum(grad_y)),
            expand_sum,
            spread(column_sum(grad_keyval_rows)[head_size:]),
        ],
        axis=1,
    )
    sums = jnp.sum(lax.all_to_all(sums, BOTH, 0, 0), axis=0)
    small_grads = []
    at = 0
    for count in lengths_of:
        small_grads.append(sums[at : at + count])
        at += count
    return (
        result,
        grad_tokens.reshape(micro, block, width),
        small_grads[0],
        small_grads[1],
        grad_query_weight,
        small_grads[2],
        grad_keyval_weight,
        small_grads[8],
        grad_out,
        small_grads[3],
        small_grads[4],
        small_grads[5],
        grad_expand,
        small_grads[7],
        grad_contract,
        small_grads[6],
    )


def solution(mesh):
    split = P(BOTH)
    rows = P(BOTH, None)
    moved = P("dp", "seq", None)
    return jax.shard_map(
        functools.partial(shards, mesh.shape["dp"], mesh.shape["seq"]),
        mesh=mesh,
        in_specs=(
            moved,
            moved,
            P(),
            P(),
            split,
            split,
            rows,
            split,
            rows,
            split,
            rows,
            split,
            split,
            split,
            rows,
            split,
            rows,
            split,
        ),
        out_specs=(
            moved,
            moved,
            split,
            split,
            rows,
            split,
            rows,
            split,
            rows,
            split,
            split,
            split,
            rows,
            split,
            rows,
            split,
        ),
        check_vma=False,
    )
```

```python
import functools
import math

import jax
import jax.numpy as jnp
from jax import lax
from jax.experimental import pallas as pl
from jax.experimental.pallas import tpu as pltpu
from jax.sharding import PartitionSpec as P

norm_eps = 1e-05
f32 = jnp.float32
bf16 = jnp.bfloat16
BOTH = ("dp", "seq")


def norm_rows(hidden):
    mean = jnp.mean(hidden, axis=1, keepdims=True)
    centered = hidden - mean
    inv_std = lax.rsqrt(jnp.mean(centered * centered, axis=1, keepdims=True) + norm_eps)
    return (centered * inv_std, inv_std)


def norm_back(grad_normed, normed, inv_std):
    mean_grad = jnp.mean(grad_normed, axis=1, keepdims=True)
    mean_proj = jnp.mean(grad_normed * normed, axis=1, keepdims=True)
    return inv_std * (grad_normed - mean_grad - normed * mean_proj)


def dot(left, right):
    return jnp.dot(left, right, preferred_element_type=f32)


def dot_general(left, right, left_dims, right_dims):
    return lax.dot_general(
        left, right, ((left_dims, right_dims), ((), ())), preferred_element_type=f32
    )


def shift(count, by):
    return [(i, (i + by) % count) for i in range(count)]


def count_of(values):
    return lax.convert_element_type(values, jnp.uint32)


def turned(me, count):
    turns = lax.rem(me + jnp.asarray([count - by for by in range(count)], jnp.uint32), count_of(count))
    return [turns[by] for by in range(count)]


def pick(values, at, axis=0):
    return lax.dynamic_index_in_dim(values, at, axis, keepdims=False)


def after(value, *gates):
    return lax.optimization_barrier((value,) + gates)[0]


def gather_parts(piece, behind):
    count = len(behind)
    whole = [piece]
    for by in range(1, count):
        whole.append(lax.ppermute(piece, "dp", shift(count, by)))
    return in_order(whole, behind)


def in_order(pieces, behind):
    whole = jnp.zeros((len(pieces),) + pieces[0].shape, pieces[0].dtype)
    for piece, at in zip(pieces, behind):
        whole = lax.dynamic_update_index_in_dim(whole, piece, at, 0)
    return whole


def ring_pieces(piece, steps, count):
    pieces = [piece]
    for step in range(1, steps):
        pieces.append(lax.ppermute(pieces[-1], "dp", shift(count, 1)))
    return pieces


def strip_routes(parts, ranks, by):
    return [(r, (r % parts + by) % parts * ranks + r // parts) for r in range(parts * ranks)]


def deal_strips(piece_for, ranks, behind, gates=()):
    parts = len(behind)
    moved = []
    for by in range(parts):
        routes = strip_routes(parts, ranks, by)
        moved.append(after(lax.ppermute(piece_for(by), BOTH, routes), *gates))
    moved = in_order(moved, behind)
    return moved.reshape((-1,) + moved.shape[2:])


def exchange_parts(pieces, ahead, behind, gates):
    count = len(behind)
    size = pieces.shape[2]
    moved = [pick(pieces, ahead[0])]
    for by in range(1, count):
        moved.append(after(lax.ppermute(pick(pieces, ahead[by]), "dp", shift(count, by)), *gates))
    whole = jnp.zeros((pieces.shape[1], count * size), pieces.dtype)
    for piece, at in zip(moved, behind):
        whole = lax.dynamic_update_slice_in_dim(whole, piece, at * count_of(size), 1)
    return whole


def ring_sum(part_for, count, gates=()):
    moving = None
    sent = ()
    for step in range(count):
        total = part_for((1 + step) % count, sent)
        if moving is not None:
            gate = gates[step - 1]() if step <= len(gates) else ()
            if gate:
                moving = after(moving, *gate)
            total = total + moving.astype(f32)
        if step < count - 1:
            sent = (total.astype(bf16),)
            moving = lax.ppermute(sent[0], "dp", shift(count, 1))
    return total


def ring_scatter(parts, behind, gates=(), all_sent=None):
    def part_for(by, sent):
        if all_sent is not None:
            all_sent.extend(sent)
        return pick(parts, behind[by]).astype(f32)

    return ring_sum(part_for, len(behind), gates)


def block_probs(query, key, limit, scale):
    raw = dot_general(query, key, (1,), (1,)) * scale
    place = lax.broadcasted_iota(jnp.int32, raw.shape, 1)
    masked = jnp.where(place <= limit, raw, -1e30)
    top = jnp.max(masked, axis=1, keepdims=True)
    unnormed = jnp.exp(masked - top)
    return unnormed / jnp.sum(unnormed, axis=1, keepdims=True)


def row_limit(first, rows, length):
    place = first + lax.broadcasted_iota(jnp.int32, (rows, 1), 0)
    return jnp.minimum(place, length - 1)


def attend_kernel(rows, scale, lengths_ref, query_ref, keyval_ref, mixed_ref):
    length = lengths_ref[pl.program_id(0)]
    blocks, one, block, size = query_ref.shape
    total = blocks * block
    step = rows // block
    for at in range(total // rows):
        span = (at + 1) * rows
        query = query_ref[at * step : (at + 1) * step].reshape(rows, size)
        keyval = keyval_ref[: (at + 1) * step].reshape(span, 2 * size)
        probs = block_probs(query, keyval[:, :size], row_limit(at * rows, rows, length), scale)
        mixed = dot(probs.astype(bf16), keyval[:, size:])
        mixed_ref[at * step : (at + 1) * step] = mixed.astype(bf16).reshape(step, 1, block, size)


def attend_back_kernel(
    rows, scale, lengths_ref, query_ref, keyval_ref, grad_ref, grad_query_ref, grad_keyval_ref, sums
):
    length = lengths_ref[pl.program_id(0)]
    head = pl.program_id(1)
    blocks, one, block, size = query_ref.shape
    total = blocks * block
    step = rows // block

    @pl.when(head == 0)
    def _():
        sums[...] = jnp.zeros_like(sums)

    for at in range(total // rows):
        span = (at + 1) * rows
        query = query_ref[at * step : (at + 1) * step].reshape(rows, size)
        grad = grad_ref[at * step : (at + 1) * step].reshape(rows, size)
        keyval = keyval_ref[: (at + 1) * step].reshape(span, 2 * size)
        probs = block_probs(query, keyval[:, :size], row_limit(at * rows, rows, length), scale)
        grad_probs = dot_general(grad, keyval[:, size:], (1,), (1,))
        inner = jnp.sum(probs * grad_probs, axis=1, keepdims=True)
        grad_scores = (probs * (grad_probs - inner)).astype(bf16)
        grad_query = (dot(grad_scores, keyval[:, :size]) * scale).astype(bf16)
        grad_query_ref[at * step : (at + 1) * step] = grad_query.reshape(step, 1, block, size)
        sums[:span, :size] += dot_general(grad_scores, query, (0,), (0,)) * scale
        sums[:span, size:] += dot_general(probs.astype(bf16), grad, (0,), (0,))

    @pl.when(head == pl.num_programs(1) - 1)
    def _():
        grad_keyval_ref[...] = sums[...].astype(bf16).reshape(grad_keyval_ref.shape)


def attention_calls(shape, head_size, rows):
    blocks, micro, block, width = shape
    heads = width // head_size
    scale = 1.0 / math.sqrt(head_size)
    head_spec = pl.BlockSpec((blocks, 1, block, head_size), lambda m, h, n: (0, m, 0, h))
    keyval_spec = pl.BlockSpec((blocks, 1, block, 2 * head_size), lambda m, h, n: (0, m, 0, 0))
    area = micro * heads * (blocks * block) ** 2 * head_size
    size = blocks * micro * block * (width + 2 * head_size) * 2
    head_out = jax.ShapeDtypeStruct(shape, bf16)
    keyval_out = jax.ShapeDtypeStruct((blocks, micro, block, 2 * head_size), bf16)
    params = pltpu.CompilerParams(vmem_limit_bytes=56 * 2**20)
    forward = pl.pallas_call(
        functools.partial(attend_kernel, rows, scale),
        out_shape=head_out,
        grid_spec=pltpu.PrefetchScalarGridSpec(
            num_scalar_prefetch=1,
            grid=(micro, heads),
            in_specs=[head_spec, keyval_spec],
            out_specs=head_spec,
        ),
        compiler_params=params,
        cost_estimate=pl.CostEstimate(
            flops=4 * area, bytes_accessed=2 * size, transcendentals=area // head_size
        ),
        name="attend",
    )
    backward = pl.pallas_call(
        functools.partial(attend_back_kernel, rows, scale),
        out_shape=(head_out, keyval_out),
        grid_spec=pltpu.PrefetchScalarGridSpec(
            num_scalar_prefetch=1,
            grid=(micro, heads),
            in_specs=[head_spec, keyval_spec, head_spec],
            out_specs=[head_spec, keyval_spec],
            scratch_shapes=[pltpu.VMEM((blocks * block, 2 * head_size), f32)],
        ),
        compiler_params=params,
        cost_estimate=pl.CostEstimate(
            flops=10 * area, bytes_accessed=4 * size, transcendentals=area // head_size
        ),
        name="attend_back",
    )
    return forward, backward


def gelu_parts(value):
    root = math.sqrt(2.0 / math.pi)
    square = value * value
    bent = jnp.tanh(root * value * (1.0 + 0.044715 * square))
    active = 0.5 * value * (1.0 + bent)
    slope = 0.5 * (1.0 + bent) + 0.5 * value * (1.0 - bent * bent) * root * (
        1.0 + 3.0 * 0.044715 * square
    )
    return active, slope


def shards(
    parts,
    ranks,
    tokens,
    cotangent,
    lengths,
    owner_order,
    first_gain,
    first_bias,
    w_query,
    b_query,
    w_keyval,
    b_value,
    w_out,
    b_out,
    second_gain,
    second_bias,
    w_expand,
    b_expand,
    w_contract,
    b_contract,
):
    micro, block, width = tokens.shape
    head_size = w_keyval.shape[1] // 2
    every = parts * ranks
    rows = micro * block
    all_rows = ranks * rows
    head_cols = width // ranks
    strip = w_query.shape[0]
    hidden_strip = w_contract.shape[0]
    hidden_cols = ranks * hidden_strip
    owner = count_of(lax.axis_index("dp"))
    rank = count_of(lax.axis_index("seq"))
    behind = turned(owner, parts)
    ahead = behind[:1] + behind[:0:-1]
    strip_at = lax.rem(owner * count_of(ranks) + rank, count_of(parts))
    strip_steps = lax.rem(strip_at + jnp.arange(parts, dtype=jnp.uint32), count_of(parts))
    own_length = lax.dynamic_slice_in_dim(lengths, owner * count_of(micro), micro)
    place = lax.axis_index("seq") * block + jnp.arange(block, dtype=jnp.int32)

    seqs = jnp.arange(parts * micro, dtype=jnp.uint32)
    steps = jnp.asarray([k // micro for k in range(parts * micro)], jnp.uint32)
    inner = jnp.asarray([k % micro for k in range(parts * micro)], jnp.uint32)

    def member(back):
        return lax.rem(owner + count_of(parts) - back, count_of(parts))

    def look_up(table, at):
        return jnp.sum(jnp.where(at[:, None] == seqs[None, :], table[None, :], 0), axis=1)

    order = count_of(owner_order)
    held = member(steps) * count_of(micro) + inner
    slots = jnp.sum(jnp.where(held[:, None] == order[None, :], seqs[None, :], 0), axis=1)
    slot_step = member(lax.div(count_of(slots), count_of(micro)))
    slot_at = slot_step * count_of(micro) + lax.rem(count_of(slots), count_of(micro))
    held_lengths = look_up(lengths, held)
    wanted = count_of(look_up(order, held))
    wanted_step = member(lax.div(wanted, count_of(micro)))
    wanted_inner = lax.rem(wanted, count_of(micro))
    wanted_at = wanted_step * count_of(micro) + wanted_inner
    wanted_steps = lax.optimization_barrier([wanted_step[k] for k in range(parts * micro)])
    wanted_lengths = look_up(lengths, wanted)[:micro]

    tokens_all = lax.all_gather(tokens.reshape(rows, width), "seq", axis=0, tiled=True)
    smalls = [
        first_gain,
        first_bias,
        b_query,
        b_out,
        second_gain,
        second_bias,
        b_contract,
        b_expand,
        b_value,
    ]
    lengths_of = [item.shape[0] for item in smalls]
    pad = -sum(lengths_of) % (16 * head_size)
    packed = jnp.concatenate(smalls + [jnp.zeros((pad,), bf16)]).reshape(-1, 2 * head_size)
    packed = jnp.concatenate([w_keyval, packed], axis=0)
    packed = gather_parts(packed, behind)
    packed = jnp.broadcast_to(packed[None], (ranks,) + packed.shape)
    packed = lax.all_to_all(packed, "seq", 0, 0).transpose(1, 0, 2, 3)
    packed = packed.reshape((every,) + packed.shape[2:])
    keyval_weight = packed[:, :strip].reshape(width, 2 * head_size)
    packed = packed[:, strip:].reshape(every, -1)
    whole = []
    at = 0
    for count in lengths_of:
        whole.append(packed[:, at : at + count].astype(f32))
        at += count
    gain_one, bias_one, query_bias, out_bias, gain_two, bias_two, contract_bias = [
        item.reshape(1, width) for item in whole[:7]
    ]
    expand_bias = pick(whole[7].reshape(parts, ranks, -1), owner)
    expand_bias = expand_bias.reshape(1, hidden_cols)
    value_bias = whole[8].reshape(1, head_size)
    query_bias = pick(query_bias.reshape(ranks, 1, head_cols), rank)
    keyval_bias = jnp.concatenate([jnp.zeros_like(value_bias), value_bias], axis=1)

    sent = w_query.reshape(strip, ranks, head_cols).transpose(1, 0, 2)
    sent = lax.all_to_all(sent, "seq", 0, 0).reshape(ranks * strip, head_cols)
    query_weight = gather_parts(sent, behind).reshape(width, head_cols)
    cotangents = ring_pieces(after(cotangent, query_weight, keyval_weight), parts, parts)
    out_strip = after(w_out, query_weight, keyval_weight)
    out_rows = deal_strips(lambda by: out_strip, ranks, behind)
    out_weight = lax.all_gather(after(out_rows, tokens_all), "seq", axis=0, tiled=True)

    head_shape = (ranks, micro, block, head_cols)
    attend, attend_back = attention_calls(head_shape, head_size, 2 * block)
    normed_all, unused_std = norm_rows(after(tokens_all, out_rows).astype(f32))
    normed_in_all = after((normed_all * gain_one + bias_one).astype(bf16))
    query = (dot(normed_in_all, query_weight) + query_bias).astype(bf16)
    keyval = (dot(normed_in_all, keyval_weight) + keyval_bias).astype(bf16)
    query = after(query, cotangents[1]).reshape(head_shape)
    keyval = keyval.reshape(ranks, micro, block, 2 * head_size)
    mixed = attend(own_length, query, keyval)
    expand_strip = after(w_expand, query, keyval, out_rows)

    def expand_piece(by):
        at = strip_steps[by] * count_of(hidden_cols)
        return lax.dynamic_slice_in_dim(expand_strip, at, hidden_cols, axis=1)

    expand_rows = deal_strips(expand_piece, ranks, behind, (mixed,))
    mixed_rows = lax.all_to_all(after(mixed, cotangents[2]), "seq", 0, 0)
    mixed_rows = after(mixed_rows, *cotangents[3:])
    mixed_rows = mixed_rows.reshape(ranks, rows, head_cols)
    mixed_rows = mixed_rows.transpose(1, 0, 2).reshape(rows, width)
    expand_weight = lax.all_gather(after(expand_rows, mixed_rows), "seq", axis=0, tiled=True)
    hidden = tokens.reshape(rows, width).astype(f32)
    resid = hidden + dot(mixed_rows, out_weight) + out_bias
    normed2, inv_std2 = norm_rows(resid)
    normed2_in = (normed2 * gain_two + bias_two).astype(bf16)
    cotangents = jnp.stack(cotangents).reshape(-1, block, width)
    inside = place[None, :, None] < held_lengths[:, None, None]

    def grad_of(by):
        taken = []
        for at in range(by * micro, (by + 1) * micro):
            piece = pick(cotangents, slot_at[at])
            taken.append(jnp.where(inside[at], piece, jnp.zeros_like(piece)))
        return jnp.concatenate(taken, axis=0)

    grad_ms = [grad_of(by) for by in range(parts)]
    grad_y = grad_ms[0].astype(f32)

    normed2_ins = ring_pieces(normed2_in, parts, parts)
    expand_weight = after(expand_weight, *normed2_ins[1:3])
    actives = [None] * parts
    slopes = [None] * parts
    grad_pres = [None] * parts

    for by in range(parts):
        preact = dot(normed2_ins[by], expand_weight) + expand_bias
        active, slopes[by] = gelu_parts(preact)
        actives[by] = active.astype(bf16)
    contract_weight = lax.all_gather(after(w_contract, expand_weight), "seq", axis=0, tiled=True)
    active_all = jnp.concatenate(actives, axis=0)
    grad_m_all = jnp.concatenate(grad_ms, axis=0)
    grad_contract = dot_general(active_all, grad_m_all, (0,), (0,)).astype(bf16)
    grad_contract_all = grad_contract

    def grad_c_for(by, sent):
        sums_c.extend(sent)
        grad_active = dot_general(grad_ms[by], contract_weight, (1,), (1,))
        grad_pres[by] = (grad_active * slopes[by]).astype(bf16)
        return dot_general(grad_pres[by], expand_weight, (1,), (1,))

    outputs = [None] * parts

    def output_of(by):
        outputs[by] = dot(actives[by], contract_weight).astype(bf16)
        return outputs[by]

    gates = (
        lambda: [grad_contract_all],
        lambda: [output_of(1)],
        lambda: [output_of(2)],
    )
    sums_c = []
    grad_c = ring_sum(grad_c_for, parts, gates)
    query_weight_all = after(query_weight.T, grad_pres[1])
    query_weight_all = lax.all_gather(query_weight_all, "seq", axis=0, tiled=True)
    grad_contract = after(grad_contract_all, sums_c[-1], query_weight_all)
    grad_contract = lax.psum_scatter(grad_contract, "seq", scatter_dimension=0, tiled=True)
    for by in range(parts):
        if outputs[by] is None:
            output_of(by)
    outputs = jnp.stack(outputs).reshape(parts * micro, block, width)
    resid_rows = resid.reshape(micro, block, width)

    def output_for(by, sent):
        taken = []
        for at in range(by * micro, (by + 1) * micro):
            own = jnp.where(wanted_steps[at] == 0, pick(resid_rows, wanted_inner[at]), 0.0)
            taken.append(pick(outputs, wanted_at[at]).astype(f32) + own)
        return jnp.stack(taken)


    grad_pre_all = jnp.concatenate(grad_pres, axis=0)
    normed2_all = jnp.concatenate(normed2_ins, axis=0)

    def grad_expand(grads):
        grads = dot_general(normed2_all, grads, (0,), (0,)).astype(bf16)
        grads = grads.reshape(parts, ranks, strip, hidden_cols).transpose(1, 0, 2, 3)
        return grads.reshape(width, hidden_cols)

    grad_resid = grad_y + norm_back(grad_c * gain_two, normed2, inv_std2)
    grad_branch = grad_resid.astype(bf16)
    grad_mixed = dot_general(grad_branch, out_weight, (1,), (1,)).astype(bf16)
    grad_mixed = grad_mixed.reshape(rows, ranks, head_cols).transpose(1, 0, 2)
    grad_mixed = lax.all_to_all(grad_mixed, "seq", 0, 0).reshape(head_shape)
    first_output = output_for(1, ()).astype(bf16)
    grad_mixed = after(grad_mixed, first_output)
    grad_query, grad_keyval = attend_back(own_length, query, keyval, grad_mixed)
    grad_branch_all = after(grad_branch, grad_mixed, grad_contract)
    grad_branch_all = lax.all_gather(grad_branch_all, "seq", axis=0, tiled=True)

    both = jnp.concatenate([grad_query, grad_keyval], axis=3)
    both_rows = lax.all_to_all(both.reshape(ranks, rows, -1), "seq", 0, 0)
    moved = after(lax.ppermute(first_output, "dp", shift(parts, 1)), grad_query)
    result = output_for(2, ()) + moved.astype(f32)
    second = result
    moved = lax.ppermute(result.astype(bf16), "dp", shift(parts, 1))
    result = output_for(3, ()) + moved.astype(f32)
    both_rows = after(both_rows, result)
    grad_branch_all = after(grad_branch_all, both_rows)
    grad_expand_all = grad_expand(after(grad_pre_all, second))
    grad_expand = after(grad_expand_all, grad_branch_all)
    grad_expand = lax.psum_scatter(grad_expand, "seq", scatter_dimension=0, tiled=True)
    both = both.reshape(all_rows, -1)
    grad_query_rows = both_rows[:, :, :head_cols].transpose(1, 0, 2).reshape(rows, width)
    grad_keyval_rows = jnp.sum(both_rows[:, :, head_cols:].astype(f32), axis=0).astype(bf16)
    grad_in = dot(grad_query_rows, query_weight_all)
    grad_in = grad_in + dot_general(grad_keyval_rows, keyval_weight, (1,), (1,))
    grad_in_weight = after(dot_general(normed_in_all, both, (0,), (0,)))
    grad_in_weight = grad_in_weight.reshape(parts, ranks * strip, both.shape[1])
    grad_out = dot_general(mixed.reshape(all_rows, head_cols), grad_branch_all, (0,), (0,))
    grad_out = grad_out.reshape(parts, head_cols // parts, width)
    sums_out = []
    grad_out = ring_scatter(grad_out, behind, [lambda: [grad_in]], sums_out)
    grad_expand = grad_expand.reshape(parts, strip, hidden_cols)
    grad_expand = exchange_parts(grad_expand, ahead, behind, (grad_in,))
    gates = [lambda: [grad_in], lambda: [sums_out[0]]]
    gates += [lambda: []] * (parts - 4) + [lambda: [grad_expand]]
    grad_in_weight = ring_scatter(grad_in_weight, behind, gates).astype(bf16)
    grad_in_weight = lax.all_to_all(
        grad_in_weight.reshape(ranks, strip, both.shape[1]), "seq", 0, 0
    )
    grad_query_weight = (
        grad_in_weight[:, :, :head_cols].transpose(1, 0, 2).reshape(strip, width).astype(f32)
    )
    grad_keyval_weight = jnp.sum(grad_in_weight[:, :, head_cols:].astype(f32), axis=0)

    back = [(d * ranks + s, s * parts + d) for d in range(parts) for s in range(ranks)]
    grad_out = lax.ppermute(grad_out.astype(bf16), BOTH, back).astype(f32)

    for step in range(4, parts + 1):
        moved = after(lax.ppermute(result.astype(bf16), "dp", shift(parts, 1)), grad_in)
        result = output_for(step % parts, ()) + moved.astype(f32)
        if step == 4:
            third = result
    held_valid = (place[None, :] < wanted_lengths[:, None])[:, :, None]
    result = jnp.where(held_valid, result + contract_bias, 0.0).astype(bf16)
    normed, inv_std = norm_rows(hidden)
    grad_tokens = grad_resid + norm_back(grad_in * gain_one, normed, inv_std)

    def spread(values):
        return values.reshape(every, -1)

    def column_sum(values):
        return jnp.sum(values.astype(f32), axis=0)

    expand_sum = column_sum(grad_pre_all).reshape(1, ranks, hidden_strip)
    here = jnp.arange(parts, dtype=jnp.uint32)[:, None, None] == owner
    expand_sum = jnp.where(here, expand_sum, 0.0).reshape(every, hidden_strip)
    sums = jnp.concatenate(
        [
            spread(column_sum(grad_in * normed)),
            spread(column_sum(grad_in)),
            spread(column_sum(grad_query_rows)),
            spread(column_sum(grad_branch)),
            spread(column_sum(grad_c * normed2)),
            spread(column_sum(grad_c)),
            spread(column_sum(grad_y)),
            expand_sum,
            spread(column_sum(grad_keyval_rows)[head_size:]),
        ],
        axis=1,
    )
    sums = jnp.sum(after(lax.all_to_all(sums, BOTH, 0, 0), grad_in_weight, third), axis=0)
    small_grads = []
    at = 0
    for count in lengths_of:
        small_grads.append(sums[at : at + count])
        at += count
    return (
        result,
        grad_tokens.reshape(micro, block, width),
        small_grads[0],
        small_grads[1],
        grad_query_weight,
        small_grads[2],
        grad_keyval_weight,
        small_grads[8],
        grad_out,
        small_grads[3],
        small_grads[4],
        small_grads[5],
        grad_expand.astype(f32),
        small_grads[7],
        after(grad_contract, grad_in).astype(f32),
        small_grads[6],
    )


def solution(mesh):
    split = P(BOTH)
    rows = P(BOTH, None)
    moved = P("dp", "seq", None)
    return jax.shard_map(
        functools.partial(shards, mesh.shape["dp"], mesh.shape["seq"]),
        mesh=mesh,
        in_specs=(
            moved,
            moved,
            P(),
            P(),
            split,
            split,
            rows,
            split,
            rows,
            split,
            rows,
            split,
            split,
            split,
            rows,
            split,
            rows,
            split,
        ),
        out_specs=(
            moved,
            moved,
            split,
            split,
            rows,
            split,
            rows,
            split,
            rows,
            split,
            split,
            split,
            rows,
            split,
            rows,
            split,
        ),
        check_vma=False,
    )
```

```python
import functools
import math

import jax
import jax.numpy as jnp
from jax import lax
from jax.experimental import pallas as pl
from jax.experimental.pallas import tpu as pltpu
from jax.sharding import PartitionSpec as P

norm_eps = 1e-05
f32 = jnp.float32
bf16 = jnp.bfloat16
BOTH = ("dp", "seq")


def norm_rows(hidden):
    mean = jnp.mean(hidden, axis=1, keepdims=True)
    centered = hidden - mean
    inv_std = lax.rsqrt(jnp.mean(centered * centered, axis=1, keepdims=True) + norm_eps)
    return (centered * inv_std, inv_std)


def norm_back(grad_normed, normed, inv_std):
    mean_grad = jnp.mean(grad_normed, axis=1, keepdims=True)
    mean_proj = jnp.mean(grad_normed * normed, axis=1, keepdims=True)
    return inv_std * (grad_normed - mean_grad - normed * mean_proj)


def dot(left, right):
    return jnp.dot(left, right, preferred_element_type=f32)


def dot_general(left, right, left_dims, right_dims):
    return lax.dot_general(
        left, right, ((left_dims, right_dims), ((), ())), preferred_element_type=f32
    )


def shift(count, by):
    return [(i, (i + by) % count) for i in range(count)]


def count_of(values):
    return lax.convert_element_type(values, jnp.uint32)


def turned(me, count):
    turns = lax.rem(me + jnp.asarray([count - by for by in range(count)], jnp.uint32), count_of(count))
    return [turns[by] for by in range(count)]


def pick(values, at, axis=0):
    return lax.dynamic_index_in_dim(values, at, axis, keepdims=False)


def after(value, *gates):
    return lax.optimization_barrier((value,) + gates)[0]


def gather_parts(piece, behind):
    count = len(behind)
    whole = [piece]
    for by in range(1, count):
        whole.append(lax.ppermute(piece, "dp", shift(count, by)))
    return in_order(whole, behind)


def in_order(pieces, behind):
    whole = jnp.zeros((len(pieces),) + pieces[0].shape, pieces[0].dtype)
    for piece, at in zip(pieces, behind):
        whole = lax.dynamic_update_index_in_dim(whole, piece, at, 0)
    return whole


def ring_pieces(piece, steps, count):
    pieces = [piece]
    for step in range(1, steps):
        pieces.append(lax.ppermute(pieces[-1], "dp", shift(count, 1)))
    return pieces


def strip_routes(parts, ranks, by):
    return [(r, (r % parts + by) % parts * ranks + r // parts) for r in range(parts * ranks)]


def deal_strips(piece_for, ranks, behind, gates=()):
    parts = len(behind)
    moved = []
    for by in range(parts):
        routes = strip_routes(parts, ranks, by)
        moved.append(after(lax.ppermute(piece_for(by), BOTH, routes), *gates))
    moved = in_order(moved, behind)
    return moved.reshape((-1,) + moved.shape[2:])


def exchange_parts(pieces, ahead, behind, gates):
    count = len(behind)
    size = pieces.shape[2]
    moved = [pick(pieces, ahead[0])]
    for by in range(1, count):
        moved.append(after(lax.ppermute(pick(pieces, ahead[by]), "dp", shift(count, by)), *gates))
    whole = jnp.zeros((pieces.shape[1], count * size), pieces.dtype)
    for piece, at in zip(moved, behind):
        whole = lax.dynamic_update_slice_in_dim(whole, piece, at * count_of(size), 1)
    return whole


def ring_sum(part_for, count, gates=()):
    moving = None
    sent = ()
    for step in range(count):
        total = part_for((1 + step) % count, sent)
        if moving is not None:
            gate = gates[step - 1]() if step <= len(gates) else ()
            if gate:
                moving = after(moving, *gate)
            total = total + moving.astype(f32)
        if step < count - 1:
            sent = (total.astype(bf16),)
            moving = lax.ppermute(sent[0], "dp", shift(count, 1))
    return total


def ring_scatter(parts, behind, gates=(), all_sent=None):
    def part_for(by, sent):
        if all_sent is not None:
            all_sent.extend(sent)
        return pick(parts, behind[by]).astype(f32)

    return ring_sum(part_for, len(behind), gates)


def block_probs(query, key, limit, scale):
    raw = dot_general(query, key, (1,), (1,)) * scale
    place = lax.broadcasted_iota(jnp.int32, raw.shape, 1)
    masked = jnp.where(place <= limit, raw, -1e30)
    top = jnp.max(masked, axis=1, keepdims=True)
    unnormed = jnp.exp(masked - top)
    return unnormed / jnp.sum(unnormed, axis=1, keepdims=True)


def row_limit(first, rows, length):
    place = first + lax.broadcasted_iota(jnp.int32, (rows, 1), 0)
    return jnp.minimum(place, length - 1)


def attend_kernel(rows, scale, lengths_ref, query_ref, keyval_ref, mixed_ref):
    length = lengths_ref[pl.program_id(0)]
    blocks, one, block, size = query_ref.shape
    total = blocks * block
    step = rows // block
    for at in range(total // rows):
        span = (at + 1) * rows
        query = query_ref[at * step : (at + 1) * step].reshape(rows, size)
        keyval = keyval_ref[: (at + 1) * step].reshape(span, 2 * size)
        probs = block_probs(query, keyval[:, :size], row_limit(at * rows, rows, length), scale)
        mixed = dot(probs.astype(bf16), keyval[:, size:])
        mixed_ref[at * step : (at + 1) * step] = mixed.astype(bf16).reshape(step, 1, block, size)


def attend_back_kernel(
    rows, scale, lengths_ref, query_ref, keyval_ref, grad_ref, grad_query_ref, grad_keyval_ref, sums
):
    length = lengths_ref[pl.program_id(0)]
    head = pl.program_id(1)
    blocks, one, block, size = query_ref.shape
    total = blocks * block
    step = rows // block

    @pl.when(head == 0)
    def _():
        sums[...] = jnp.zeros_like(sums)

    for at in range(total // rows):
        span = (at + 1) * rows
        query = query_ref[at * step : (at + 1) * step].reshape(rows, size)
        grad = grad_ref[at * step : (at + 1) * step].reshape(rows, size)
        keyval = keyval_ref[: (at + 1) * step].reshape(span, 2 * size)
        probs = block_probs(query, keyval[:, :size], row_limit(at * rows, rows, length), scale)
        grad_probs = dot_general(grad, keyval[:, size:], (1,), (1,))
        inner = jnp.sum(probs * grad_probs, axis=1, keepdims=True)
        grad_scores = (probs * (grad_probs - inner)).astype(bf16)
        grad_query = (dot(grad_scores, keyval[:, :size]) * scale).astype(bf16)
        grad_query_ref[at * step : (at + 1) * step] = grad_query.reshape(step, 1, block, size)
        sums[:span, :size] += dot_general(grad_scores, query, (0,), (0,)) * scale
        sums[:span, size:] += dot_general(probs.astype(bf16), grad, (0,), (0,))

    @pl.when(head == pl.num_programs(1) - 1)
    def _():
        grad_keyval_ref[...] = sums[...].astype(bf16).reshape(grad_keyval_ref.shape)


def attention_calls(shape, head_size, rows):
    blocks, micro, block, width = shape
    heads = width // head_size
    scale = 1.0 / math.sqrt(head_size)
    head_spec = pl.BlockSpec((blocks, 1, block, head_size), lambda m, h, n: (0, m, 0, h))
    keyval_spec = pl.BlockSpec((blocks, 1, block, 2 * head_size), lambda m, h, n: (0, m, 0, 0))
    area = micro * heads * (blocks * block) ** 2 * head_size
    size = blocks * micro * block * (width + 2 * head_size) * 2
    head_out = jax.ShapeDtypeStruct(shape, bf16)
    keyval_out = jax.ShapeDtypeStruct((blocks, micro, block, 2 * head_size), bf16)
    params = pltpu.CompilerParams(vmem_limit_bytes=56 * 2**20)
    forward = pl.pallas_call(
        functools.partial(attend_kernel, rows, scale),
        out_shape=head_out,
        grid_spec=pltpu.PrefetchScalarGridSpec(
            num_scalar_prefetch=1,
            grid=(micro, heads),
            in_specs=[head_spec, keyval_spec],
            out_specs=head_spec,
        ),
        compiler_params=params,
        cost_estimate=pl.CostEstimate(
            flops=4 * area, bytes_accessed=2 * size, transcendentals=area // head_size
        ),
        name="attend",
    )
    backward = pl.pallas_call(
        functools.partial(attend_back_kernel, rows, scale),
        out_shape=(head_out, keyval_out),
        grid_spec=pltpu.PrefetchScalarGridSpec(
            num_scalar_prefetch=1,
            grid=(micro, heads),
            in_specs=[head_spec, keyval_spec, head_spec],
            out_specs=[head_spec, keyval_spec],
            scratch_shapes=[pltpu.VMEM((blocks * block, 2 * head_size), f32)],
        ),
        compiler_params=params,
        cost_estimate=pl.CostEstimate(
            flops=10 * area, bytes_accessed=4 * size, transcendentals=area // head_size
        ),
        name="attend_back",
    )
    return forward, backward


def gelu_parts(value):
    root = math.sqrt(2.0 / math.pi)
    square = value * value
    bent = jnp.tanh(root * value * (1.0 + 0.044715 * square))
    active = 0.5 * value * (1.0 + bent)
    slope = 0.5 * (1.0 + bent) + 0.5 * value * (1.0 - bent * bent) * root * (
        1.0 + 3.0 * 0.044715 * square
    )
    return active, slope


def shards(
    parts,
    ranks,
    tokens,
    cotangent,
    lengths,
    owner_order,
    first_gain,
    first_bias,
    w_query,
    b_query,
    w_keyval,
    b_value,
    w_out,
    b_out,
    second_gain,
    second_bias,
    w_expand,
    b_expand,
    w_contract,
    b_contract,
):
    micro, block, width = tokens.shape
    head_size = w_keyval.shape[1] // 2
    every = parts * ranks
    rows = micro * block
    all_rows = ranks * rows
    head_cols = width // ranks
    strip = w_query.shape[0]
    hidden_strip = w_contract.shape[0]
    hidden_cols = ranks * hidden_strip
    owner = count_of(lax.axis_index("dp"))
    rank = count_of(lax.axis_index("seq"))
    behind = turned(owner, parts)
    ahead = behind[:1] + behind[:0:-1]
    strip_at = lax.rem(owner * count_of(ranks) + rank, count_of(parts))
    strip_steps = lax.rem(strip_at + jnp.arange(parts, dtype=jnp.uint32), count_of(parts))
    own_length = lax.dynamic_slice_in_dim(lengths, owner * count_of(micro), micro)
    place = lax.axis_index("seq") * block + jnp.arange(block, dtype=jnp.int32)

    seqs = jnp.arange(parts * micro, dtype=jnp.uint32)
    steps = jnp.asarray([k // micro for k in range(parts * micro)], jnp.uint32)
    inner = jnp.asarray([k % micro for k in range(parts * micro)], jnp.uint32)

    def member(back):
        return lax.rem(owner + count_of(parts) - back, count_of(parts))

    def look_up(table, at):
        return jnp.sum(jnp.where(at[:, None] == seqs[None, :], table[None, :], 0), axis=1)

    order = count_of(owner_order)
    held = member(steps) * count_of(micro) + inner
    slots = jnp.sum(jnp.where(held[:, None] == order[None, :], seqs[None, :], 0), axis=1)
    slot_step = member(lax.div(count_of(slots), count_of(micro)))
    slot_at = slot_step * count_of(micro) + lax.rem(count_of(slots), count_of(micro))
    held_lengths = look_up(lengths, held)
    wanted = count_of(look_up(order, held))
    wanted_step = member(lax.div(wanted, count_of(micro)))
    wanted_inner = lax.rem(wanted, count_of(micro))
    wanted_at = wanted_step * count_of(micro) + wanted_inner
    wanted_steps = lax.optimization_barrier([wanted_step[k] for k in range(parts * micro)])
    wanted_lengths = look_up(lengths, wanted)[:micro]

    tokens_all = lax.all_gather(tokens.reshape(rows, width), "seq", axis=0, tiled=True)
    smalls = [
        first_gain,
        first_bias,
        b_query,
        b_out,
        second_gain,
        second_bias,
        b_contract,
        b_expand,
        b_value,
    ]
    lengths_of = [item.shape[0] for item in smalls]
    pad = -sum(lengths_of) % (16 * head_size)
    packed = jnp.concatenate(smalls + [jnp.zeros((pad,), bf16)]).reshape(-1, 2 * head_size)
    packed = jnp.concatenate([w_keyval, packed], axis=0)
    packed = gather_parts(packed, behind)
    packed = jnp.broadcast_to(packed[None], (ranks,) + packed.shape)
    packed = lax.all_to_all(packed, "seq", 0, 0).transpose(1, 0, 2, 3)
    packed = packed.reshape((every,) + packed.shape[2:])
    keyval_weight = packed[:, :strip].reshape(width, 2 * head_size)
    packed = packed[:, strip:].reshape(every, -1)
    whole = []
    at = 0
    for count in lengths_of:
        whole.append(packed[:, at : at + count].astype(f32))
        at += count
    gain_one, bias_one, query_bias, out_bias, gain_two, bias_two, contract_bias = [
        item.reshape(1, width) for item in whole[:7]
    ]
    expand_bias = pick(whole[7].reshape(parts, ranks, -1), owner)
    expand_bias = expand_bias.reshape(1, hidden_cols)
    value_bias = whole[8].reshape(1, head_size)
    query_bias = pick(query_bias.reshape(ranks, 1, head_cols), rank)
    keyval_bias = jnp.concatenate([jnp.zeros_like(value_bias), value_bias], axis=1)

    sent = w_query.reshape(strip, ranks, head_cols).transpose(1, 0, 2)
    sent = lax.all_to_all(sent, "seq", 0, 0).reshape(ranks * strip, head_cols)
    query_weight = gather_parts(sent, behind).reshape(width, head_cols)
    cotangents = ring_pieces(after(cotangent, query_weight, keyval_weight), parts, parts)
    out_strip = after(w_out, query_weight, keyval_weight)
    out_rows = deal_strips(lambda by: out_strip, ranks, behind)
    out_weight = lax.all_gather(after(out_rows, tokens_all), "seq", axis=0, tiled=True)

    head_shape = (ranks, micro, block, head_cols)
    attend, attend_back = attention_calls(head_shape, head_size, 2 * block)
    normed_all, unused_std = norm_rows(after(tokens_all, out_rows).astype(f32))
    normed_in_all = after((normed_all * gain_one + bias_one).astype(bf16))
    query = (dot(normed_in_all, query_weight) + query_bias).astype(bf16)
    keyval = (dot(normed_in_all, keyval_weight) + keyval_bias).astype(bf16)
    query = after(query, cotangents[1]).reshape(head_shape)
    keyval = keyval.reshape(ranks, micro, block, 2 * head_size)
    mixed = attend(own_length, query, keyval)
    expand_strip = after(w_expand, query, keyval, out_rows)

    def expand_piece(by):
        at = strip_steps[by] * count_of(hidden_cols)
        return lax.dynamic_slice_in_dim(expand_strip, at, hidden_cols, axis=1)

    expand_rows = deal_strips(expand_piece, ranks, behind, (mixed,))
    mixed_rows = lax.all_to_all(after(mixed, cotangents[2]), "seq", 0, 0)
    mixed_rows = after(mixed_rows, *cotangents[3:])
    mixed_rows = mixed_rows.reshape(ranks, rows, head_cols)
    mixed_rows = mixed_rows.transpose(1, 0, 2).reshape(rows, width)
    expand_weight = lax.all_gather(after(expand_rows, mixed_rows), "seq", axis=0, tiled=True)
    hidden = tokens.reshape(rows, width).astype(f32)
    resid = hidden + dot(mixed_rows, out_weight) + out_bias
    normed2, inv_std2 = norm_rows(resid)
    normed2_in = (normed2 * gain_two + bias_two).astype(bf16)
    cotangents = jnp.stack(cotangents).reshape(-1, block, width)
    inside = place[None, :, None] < held_lengths[:, None, None]

    def grad_of(by):
        taken = []
        for at in range(by * micro, (by + 1) * micro):
            piece = pick(cotangents, slot_at[at])
            taken.append(jnp.where(inside[at], piece, jnp.zeros_like(piece)))
        return jnp.concatenate(taken, axis=0)

    grad_ms = [grad_of(by) for by in range(parts)]
    grad_y = grad_ms[0].astype(f32)

    normed2_ins = ring_pieces(normed2_in, parts, parts)
    expand_weight = after(expand_weight, *normed2_ins[1:3])
    actives = [None] * parts
    slopes = [None] * parts
    grad_pres = [None] * parts

    sums_c = []

    def forward(by, *gates):
        preact = dot(after(normed2_ins[by], *gates), expand_weight) + expand_bias
        active, slopes[by] = gelu_parts(preact)
        actives[by] = active.astype(bf16)

    for by in range(3):
        forward(by)
    contract_weight = lax.all_gather(after(w_contract, expand_weight), "seq", axis=0, tiled=True)
    grad_m_all = jnp.concatenate(grad_ms, axis=0)
    grad_contracts = []

    def contract_gate():
        active_all = jnp.concatenate(actives, axis=0)
        grad_contracts.append(dot_general(active_all, grad_m_all, (0,), (0,)).astype(bf16))
        return grad_contracts

    def grad_c_for(by, sent):
        sums_c.extend(sent)
        if actives[by] is None:
            forward(by, *sums_c[:1])
        grad_active = dot_general(grad_ms[by], contract_weight, (1,), (1,))
        grad_pres[by] = (grad_active * slopes[by]).astype(bf16)
        return dot_general(grad_pres[by], expand_weight, (1,), (1,))

    outputs = [None] * parts

    def output_of(by):
        outputs[by] = dot(actives[by], contract_weight).astype(bf16)
        return outputs[by]

    gates = (
        lambda: [output_of(1)],
        *[lambda: []] * (parts - 4),
        contract_gate,
        lambda: [output_of(2)],
    )
    grad_c = ring_sum(grad_c_for, parts, gates)
    query_weight_all = after(query_weight.T, grad_pres[1])
    query_weight_all = lax.all_gather(query_weight_all, "seq", axis=0, tiled=True)
    grad_contract = after(grad_contracts[0], query_weight_all)
    grad_contract = lax.psum_scatter(grad_contract, "seq", scatter_dimension=0, tiled=True)
    for by in range(parts):
        if outputs[by] is None:
            output_of(by)
    outputs = jnp.stack(outputs).reshape(parts * micro, block, width)
    resid_rows = resid.reshape(micro, block, width)

    def output_for(by, sent):
        taken = []
        for at in range(by * micro, (by + 1) * micro):
            own = jnp.where(wanted_steps[at] == 0, pick(resid_rows, wanted_inner[at]), 0.0)
            taken.append(pick(outputs, wanted_at[at]).astype(f32) + own)
        return jnp.stack(taken)


    grad_pre_all = jnp.concatenate(grad_pres, axis=0)
    normed2_all = jnp.concatenate(normed2_ins, axis=0)

    def grad_expand(grads):
        grads = dot_general(normed2_all, grads, (0,), (0,)).astype(bf16)
        grads = grads.reshape(parts, ranks, strip, hidden_cols).transpose(1, 0, 2, 3)
        return grads.reshape(width, hidden_cols)

    grad_resid = grad_y + norm_back(grad_c * gain_two, normed2, inv_std2)
    grad_branch = grad_resid.astype(bf16)
    grad_mixed = dot_general(grad_branch, out_weight, (1,), (1,)).astype(bf16)
    grad_mixed = grad_mixed.reshape(rows, ranks, head_cols).transpose(1, 0, 2)
    grad_mixed = lax.all_to_all(grad_mixed, "seq", 0, 0).reshape(head_shape)
    first_output = output_for(1, ()).astype(bf16)
    grad_mixed = after(grad_mixed, first_output)
    grad_query, grad_keyval = attend_back(own_length, query, keyval, grad_mixed)
    grad_branch_all = after(grad_branch, grad_mixed, grad_contract)
    grad_branch_all = lax.all_gather(grad_branch_all, "seq", axis=0, tiled=True)

    both = jnp.concatenate([grad_query, grad_keyval], axis=3)
    both_rows = lax.all_to_all(both.reshape(ranks, rows, -1), "seq", 0, 0)
    moved = after(lax.ppermute(first_output, "dp", shift(parts, 1)), grad_query)
    result = output_for(2, ()) + moved.astype(f32)
    second = result
    moved = lax.ppermute(result.astype(bf16), "dp", shift(parts, 1))
    result = output_for(3, ()) + moved.astype(f32)
    both_rows = after(both_rows, result)
    grad_branch_all = after(grad_branch_all, both_rows)
    grad_expand_all = grad_expand(after(grad_pre_all, second))
    grad_expand = after(grad_expand_all, grad_branch_all)
    grad_expand = lax.psum_scatter(grad_expand, "seq", scatter_dimension=0, tiled=True)
    both = both.reshape(all_rows, -1)
    grad_query_rows = both_rows[:, :, :head_cols].transpose(1, 0, 2).reshape(rows, width)
    grad_keyval_rows = jnp.sum(both_rows[:, :, head_cols:].astype(f32), axis=0).astype(bf16)
    grad_in = dot(grad_query_rows, query_weight_all)
    grad_in = grad_in + dot_general(grad_keyval_rows, keyval_weight, (1,), (1,))
    grad_in_weight = after(dot_general(normed_in_all, both, (0,), (0,)))
    grad_in_weight = grad_in_weight.reshape(parts, ranks * strip, both.shape[1])
    grad_out = dot_general(mixed.reshape(all_rows, head_cols), grad_branch_all, (0,), (0,))
    grad_out = grad_out.reshape(parts, head_cols // parts, width)
    sums_out = []
    grad_out = ring_scatter(grad_out, behind, [lambda: [grad_in]], sums_out)
    grad_expand = grad_expand.reshape(parts, strip, hidden_cols)
    grad_expand = exchange_parts(grad_expand, ahead, behind, (grad_in,))
    gates = [lambda: [grad_in], lambda: [sums_out[0]]]
    gates += [lambda: []] * (parts - 4) + [lambda: [grad_expand]]
    grad_in_weight = ring_scatter(grad_in_weight, behind, gates).astype(bf16)
    grad_in_weight = lax.all_to_all(
        grad_in_weight.reshape(ranks, strip, both.shape[1]), "seq", 0, 0
    )
    grad_query_weight = (
        grad_in_weight[:, :, :head_cols].transpose(1, 0, 2).reshape(strip, width).astype(f32)
    )
    grad_keyval_weight = jnp.sum(grad_in_weight[:, :, head_cols:].astype(f32), axis=0)

    back = [(d * ranks + s, s * parts + d) for d in range(parts) for s in range(ranks)]
    grad_out = lax.ppermute(grad_out.astype(bf16), BOTH, back).astype(f32)

    for step in range(4, parts + 1):
        moved = after(lax.ppermute(result.astype(bf16), "dp", shift(parts, 1)), grad_in)
        result = output_for(step % parts, ()) + moved.astype(f32)
        if step == 4:
            third = result
    held_valid = (place[None, :] < wanted_lengths[:, None])[:, :, None]
    result = jnp.where(held_valid, result + contract_bias, 0.0).astype(bf16)
    normed, inv_std = norm_rows(hidden)
    grad_tokens = grad_resid + norm_back(grad_in * gain_one, normed, inv_std)

    def spread(values):
        return values.reshape(every, -1)

    def column_sum(values):
        return jnp.sum(values.astype(f32), axis=0)

    expand_sum = column_sum(grad_pre_all).reshape(1, ranks, hidden_strip)
    here = jnp.arange(parts, dtype=jnp.uint32)[:, None, None] == owner
    expand_sum = jnp.where(here, expand_sum, 0.0).reshape(every, hidden_strip)
    sums = jnp.concatenate(
        [
            spread(column_sum(grad_in * normed)),
            spread(column_sum(grad_in)),
            spread(column_sum(grad_query_rows)),
            spread(column_sum(grad_branch)),
            spread(column_sum(grad_c * normed2)),
            spread(column_sum(grad_c)),
            spread(column_sum(grad_y)),
            expand_sum,
            spread(column_sum(grad_keyval_rows)[head_size:]),
        ],
        axis=1,
    )
    sums = jnp.sum(after(lax.all_to_all(sums, BOTH, 0, 0), grad_in_weight, third), axis=0)
    small_grads = []
    at = 0
    for count in lengths_of:
        small_grads.append(sums[at : at + count])
        at += count
    return (
        result,
        grad_tokens.reshape(micro, block, width),
        small_grads[0],
        small_grads[1],
        grad_query_weight,
        small_grads[2],
        grad_keyval_weight,
        small_grads[8],
        grad_out,
        small_grads[3],
        small_grads[4],
        small_grads[5],
        grad_expand.astype(f32),
        small_grads[7],
        after(grad_contract, grad_in).astype(f32),
        small_grads[6],
    )


def solution(mesh):
    split = P(BOTH)
    rows = P(BOTH, None)
    moved = P("dp", "seq", None)
    return jax.shard_map(
        functools.partial(shards, mesh.shape["dp"], mesh.shape["seq"]),
        mesh=mesh,
        in_specs=(
            moved,
            moved,
            P(),
            P(),
            split,
            split,
            rows,
            split,
            rows,
            split,
            rows,
            split,
            split,
            split,
            rows,
            split,
            rows,
            split,
        ),
        out_specs=(
            moved,
            moved,
            split,
            split,
            rows,
            split,
            rows,
            split,
            rows,
            split,
            split,
            split,
            rows,
            split,
            rows,
            split,
        ),
        check_vma=False,
    )
```
